128 devices in a mesh: group: 4 (over y), member: 32 (over z, x, core).
Axes of the slice: x: 4, y: 4, z: 4, core: 2. Of those that a mesh axis runs over, the one named last changes fastest.
Arguments:
- memory: float32 [131072, 512], P(('group', 'member')), may hold values from -3 to 3
- source_owner: int32 [32768, 1], P(('group', 'member')), may hold values from 0 to 127; in each aligned block of 256 rows (0 to 255, 256 to 511, ...) at most 4 rows name the same one
- target_owner: int32 [32768, 1], P(('group', 'member')), may hold values from 0 to 127; in each aligned block of 256 rows (0 to 255, 256 to 511, ...) at most 4 rows name the same one
- source_row: int32 [32768], P(('group', 'member')), may hold values from 0 to 1023
- target_row: int32 [32768], P(('group', 'member')), may hold values from 0 to 1023
- event_time: int32 [32768], P(('group', 'member')), may hold values from 0 to 2047
- query_rows: int32 [16384], P(('group', 'member')), may hold values from 0 to 1023
- link_member: int32 [163840, 1], P(('group', 'member')), may hold values from 0 to 31; in each aligned block of 1280 rows (0 to 1279, 1280 to 2559, ...) at most 80 rows name the same one
- link_slot: int32 [163840], P(('group', 'member')), may hold values from 0 to 127
- link_delta: int32 [163840], P(('group', 'member')), may hold values from 0 to 2047
- frequency: float32 [128], replicated, may hold values from 0.001 to 0.5
- time_phase: float32 [128], replicated, may hold values from -3.140625 to 3.140625
- msg_weight: bfloat16 [1152, 512], replicated, may hold values from -0.1875 to 0.1875
- msg_bias: float32 [512], replicated, may hold values from -3 to 3
- input_weight: bfloat16 [512, 1536], replicated, may hold values from -0.25 to 0.25
- state_weight: bfloat16 [512, 1536], replicated, may hold values from -0.25 to 0.25
- input_bias: float32 [1536], replicated, may hold values from -3 to 3
- state_bias: float32 [1536], replicated, may hold values from -3 to 3
- query_weight: bfloat16 [2, 640, 512], replicated, may hold values from -0.25 to 0.25
- key_weight: bfloat16 [2, 640, 512], replicated, may hold values from -0.25 to 0.25
- value_weight: bfloat16 [2, 640, 512], replicated, may hold values from -0.25 to 0.25
- merge_weight: bfloat16 [2, 1024, 512], replicated, may hold values from -0.1875 to 0.1875
- merge_bias: float32 [2, 512], replicated, may hold values from -3 to 3
Outputs:
- new_memory: float32 [131072, 512], P(('group', 'member'))
- embedding: bfloat16 [16384, 512], P(('group', 'member'))
The draws below stay inside these ranges and needn't reach their ends.
Inputs may be any that keep to these rules, and one draw needn't show every extreme that they name: `source_owner`: among the events of one device at most 4 have their source owned by one device, and some device's events reach it. `target_owner`: among the events of one device at most 4 have their destination owned by one device, and some device's events reach it. `link_member`: among the links of one device at most 80 point to one member, and some device's links reach it.
All inputs are finite; a program needn't handle non-finite values.
Results may differ from the reference program's by a relative error of at most 0.0065.
Values may be sent and summed in bfloat16 or wider, within the bound.
A program may use at most 128 MiB of HBM per device.

```python
import math
import jax
import jax.numpy as jnp
import numpy as np
from jax import lax

M = 512
TD = 128
HEADS = 2
NB = 10
NODE_DEV = 1024
EV_DEV = 256
Q_DEV = 128
CAPE = 4
CAPN = 80
NODES = 131072
EVENTS = 32768
QUERIES = 16384
N_MEMBER = 32
DEVICES = 128


def set_ends(array, stream_key, smallest, high):
    shape = array.shape
    spot = [jax.random.randint(jax.random.fold_in(stream_key, axis), (), 0, shape[axis]) for axis in range(len(shape))]
    array = array.at[tuple(spot)].set(smallest)
    longest = shape.index(max(shape))
    spot[longest] = (spot[longest] + 1) % shape[longest]
    return array.at[tuple(spot)].set(high)


def level_of(key, extent, shards, least, high):
    factor_of, own = 1.0, jax.random.fold_in(key, 6)
    for position, parts in shards:
        draws = jnp.exp(jax.random.uniform(jax.random.fold_in(own, position), (parts,), jnp.float32, least / len(shards), high / len(shards)))
        factor_of = factor_of * jnp.repeat(draws, extent[position] // parts).reshape([-1 if axis == position else 1 for axis in range(len(extent))])
    return factor_of


def assign_block(rng, own, number, rows, amount, top, reach, slope):
    order = jax.random.permutation(rng, amount)
    crowded, common = shares(amount, rows * top, reach, slope, True), shares(amount, rows * top, reach, slope, False)
    places = jnp.arange(amount)

    def named(lengths, rotation):
        used = int((lengths > 0).sum())
        fixed = max(1, used // 4)
        shifted = fixed + (places - fixed + rotation * (used - fixed)) % max(1, amount - fixed)
        return jnp.zeros((amount,), jnp.int32).at[order[jnp.where(places < fixed, places, shifted)]].set(jnp.asarray(lengths, jnp.int32))

    lengths = jnp.where(number % 4 == 0, named(crowded, number // 4), named(common, number - number // 4 - 1))
    mixed = jax.random.permutation(jax.random.fold_in(own, 3), amount)
    giver, sink = mixed[0:amount // 2 * 2:2], mixed[1:amount // 2 * 2:2]
    room = jnp.minimum(lengths[giver] - 1, reach - lengths[sink]) // 2
    room = jnp.where((giver == order[0]) | (sink == order[0]) | (lengths[sink] == 0), 0, jnp.maximum(room, 0))
    shifted = jax.random.randint(jax.random.fold_in(own, 4), (amount // 2,), 0, 1 << 20) % (room + 1)
    lengths = lengths.at[giver].add(-shifted).at[sink].add(shifted)
    labels = jnp.searchsorted(jnp.cumsum(lengths), jnp.arange(rows * top), side="right").astype(jnp.int32)
    listing = labels.reshape(top, rows).T
    listing = listing[jax.random.permutation(jax.random.fold_in(own, 1), rows)]
    rotation = jax.random.randint(jax.random.fold_in(own, 2), (rows, 1), 0, top)
    return jnp.take_along_axis(listing, (jnp.arange(top)[None, :] + rotation) % top, axis=1)


def shares(count, total, most, slope, full):
    portions = [(1 << 20) // math.isqrt(rank ** slope) + 1 for rank in range(1, count + 1)]
    largest = most if full else min(most, max(-(-total // count), total * portions[0] // sum(portions)))
    least = 1 if total - largest >= count - 1 else 0
    counts, rest = [largest] + [least] * (count - 1), total - largest - least * (count - 1)
    while rest > 0:
        free = [i for i in range(1, count) if counts[i] < largest] or [i for i in range(1, count) if counts[i] < most]
        whole, left = sum([portions[i] for i in free]), rest
        for i in free:
            more = min(most - counts[i], max(1, left * portions[i] // whole), rest)
            counts[i] = counts[i] + more
            rest = rest - more
    return np.array(counts)


def centred(rng, extent, width, most, cuts=(), kind=jnp.bfloat16):
    result = width * jax.random.normal(rng, extent, jnp.float32)
    if cuts:
        result = result * level_of(rng, extent, cuts, -0.22, 0.18)
    return jnp.clip(result, -most, most).astype(kind)


def setup_inputs(seed: int = 0) -> dict:
    key_of = jax.random.split(jax.random.key(seed), 24)
    memory = centred(key_of[0], (NODES, M), 0.5, 3.0, ((0, 128),), jnp.float32)
    source_owner_keys = jax.random.split(jax.random.fold_in(key_of[1], 1), EVENTS // EV_DEV)
    source_owner_turns = jax.random.permutation(jax.random.fold_in(key_of[1], 3), EVENTS // EV_DEV)
    source_owner = jax.vmap(lambda own, number: assign_block(jax.random.fold_in(key_of[1], 2), own, number, EV_DEV, DEVICES, 1, CAPE, 1))(source_owner_keys, source_owner_turns).reshape((EVENTS, 1))
    target_owner_keys = jax.random.split(jax.random.fold_in(key_of[2], 1), EVENTS // EV_DEV)
    target_owner_turns = jax.random.permutation(jax.random.fold_in(key_of[2], 3), EVENTS // EV_DEV)
    target_owner = jax.vmap(lambda own, number: assign_block(jax.random.fold_in(key_of[2], 2), own, number, EV_DEV, DEVICES, 1, CAPE, 1))(target_owner_keys, target_owner_turns).reshape((EVENTS, 1))
    source_row = set_ends(jax.random.randint(key_of[3], (EVENTS,), 0, NODE_DEV), jax.random.fold_in(key_of[3], 1), 0, NODE_DEV - 1).astype(jnp.int32)
    target_row = set_ends(jax.random.randint(key_of[4], (EVENTS,), 0, NODE_DEV), jax.random.fold_in(key_of[4], 1), 0, NODE_DEV - 1).astype(jnp.int32)
    event_time = set_ends(jax.random.randint(key_of[5], (EVENTS,), 0, 2048), jax.random.fold_in(key_of[5], 1), 0, 2047).astype(jnp.int32)
    query_rows = set_ends(jax.random.randint(key_of[6], (QUERIES,), 0, NODE_DEV), jax.random.fold_in(key_of[6], 1), 0, NODE_DEV - 1).astype(jnp.int32)
    link_member_keys = jax.random.split(jax.random.fold_in(key_of[7], 1), (QUERIES * NB) // (Q_DEV * NB))
    link_member_turns = jax.random.permutation(jax.random.fold_in(key_of[7], 3), (QUERIES * NB) // (Q_DEV * NB))
    link_member = jax.vmap(lambda own, number: assign_block(jax.random.fold_in(key_of[7], 2), own, number, Q_DEV * NB, N_MEMBER, 1, CAPN, 1))(link_member_keys, link_member_turns).reshape((QUERIES * NB, 1))
    link_slot = set_ends(jax.random.randint(key_of[8], (QUERIES * NB,), 0, Q_DEV), jax.random.fold_in(key_of[8], 1), 0, Q_DEV - 1).astype(jnp.int32)
    link_delta = set_ends(jax.random.randint(key_of[9], (QUERIES * NB,), 0, 2048), jax.random.fold_in(key_of[9], 1), 0, 2047).astype(jnp.int32)
    frequency = jnp.clip(jnp.exp(jax.random.uniform(key_of[10], (TD,), jnp.float32, math.log(0.001), math.log(0.5))), 0.001, 0.5)
    time_phase = jnp.clip(jax.random.uniform(key_of[11], (TD,), jnp.float32, -3.140625, 3.140625), -3.140625, 3.140625)
    msg_weight = centred(key_of[12], (2 * M + TD, M), (2 * M + TD) ** -0.5, 0.1875)
    msg_bias = centred(key_of[13], (M,), 0.5, 3.0, (), jnp.float32)
    input_weight = centred(key_of[14], (M, 3 * M), M ** -0.5, 0.25)
    state_weight = centred(key_of[15], (M, 3 * M), M ** -0.5, 0.25)
    input_bias = centred(key_of[16], (3 * M,), 0.5, 3.0, (), jnp.float32)
    state_bias = centred(key_of[17], (3 * M,), 0.5, 3.0, (), jnp.float32)
    query_weight = centred(key_of[18], (2, M + TD, M), (M + TD) ** -0.5, 0.25)
    key_weight = centred(key_of[19], (2, M + TD, M), (M + TD) ** -0.5, 0.25)
    value_weight = centred(key_of[20], (2, M + TD, M), (M + TD) ** -0.5, 0.25)
    merge_weight = centred(key_of[21], (2, 2 * M, M), (2 * M) ** -0.5, 0.1875)
    merge_bias = centred(key_of[22], (2, M), 0.5, 3.0, (), jnp.float32)
    return dict(memory=memory, source_owner=source_owner, target_owner=target_owner, source_row=source_row, target_row=target_row, event_time=event_time, query_rows=query_rows, link_member=link_member, link_slot=link_slot, link_delta=link_delta, frequency=frequency, time_phase=time_phase, msg_weight=msg_weight, msg_bias=msg_bias, input_weight=input_weight, state_weight=state_weight, input_bias=input_bias, state_bias=state_bias, query_weight=query_weight, key_weight=key_weight, value_weight=value_weight, merge_weight=merge_weight, merge_bias=merge_bias)


def time_code(stamps, frequency, time_phase):
    return jnp.cos(stamps.astype(jnp.float32)[:, None] * frequency[None, :] + time_phase[None, :]).astype(jnp.bfloat16)

def gru_cell(inputs, hidden, input_weight, state_weight, input_bias, state_bias):
    row_width = hidden.shape[1]
    from_input = jnp.dot(inputs, input_weight, preferred_element_type=jnp.float32) + input_bias
    from_state = jnp.dot(hidden.astype(jnp.bfloat16), state_weight, preferred_element_type=jnp.float32) + state_bias
    reset_gate = jax.nn.sigmoid(from_input[:, :row_width] + from_state[:, :row_width])
    update_gate = jax.nn.sigmoid(from_input[:, row_width:2 * row_width] + from_state[:, row_width:2 * row_width])
    candidate = jnp.tanh(from_input[:, 2 * row_width:] + reset_gate * from_state[:, 2 * row_width:])
    return (1.0 - update_gate) * candidate + update_gate * hidden

def attend(feats, neighbours, delta_code, self_code, query_weight, key_weight, value_weight, merge_weight, merge_bias, head_count):
    query_count, row_width = feats.shape
    fanout = neighbours.shape[1]
    head_size = row_width // head_count
    query_vec = jnp.dot(jnp.concatenate([feats, self_code], 1), query_weight, preferred_element_type=jnp.float32)
    key_input = jnp.concatenate([neighbours, delta_code], 2).reshape(query_count * fanout, -1)
    key_vec = jnp.dot(key_input, key_weight, preferred_element_type=jnp.float32).reshape(query_count, fanout, head_count, head_size)
    value_vec = jnp.dot(key_input, value_weight, preferred_element_type=jnp.float32).reshape(query_count, fanout, head_count, head_size)
    query_vec = query_vec.reshape(query_count, 1, head_count, head_size)
    scores = lax.optimization_barrier(jnp.sum(query_vec * key_vec, axis=3)) / math.sqrt(head_size)
    weights = jnp.exp(scores)
    weights = weights / lax.optimization_barrier(jnp.sum(weights, axis=1, keepdims=True))
    mixed_out = lax.optimization_barrier(jnp.sum(weights[..., None] * value_vec, axis=1)).reshape(query_count, row_width).astype(jnp.bfloat16)
    merged = jnp.dot(jnp.concatenate([mixed_out, feats], 1), merge_weight, preferred_element_type=jnp.float32) + merge_bias
    return jax.nn.relu(merged).astype(jnp.bfloat16)

def reference(memory, source_owner, target_owner, source_row, target_row, event_time, query_rows, link_member, link_slot, link_delta, frequency, time_phase, msg_weight, msg_bias, input_weight, state_weight, input_bias, state_bias, query_weight, key_weight, value_weight, merge_weight, merge_bias):
    source_id = (source_owner[:, 0] * NODE_DEV + source_row).astype(jnp.int32)
    target_id = (target_owner[:, 0] * NODE_DEV + target_row).astype(jnp.int32)
    source_mem = memory[source_id].astype(jnp.bfloat16)
    target_mem = memory[target_id].astype(jnp.bfloat16)
    stamp_code = time_code(event_time, frequency, time_phase)
    inputs = jnp.concatenate([jnp.concatenate([source_mem, target_mem, stamp_code], 1), jnp.concatenate([target_mem, source_mem, stamp_code], 1)], 0)
    message = jax.nn.relu(jnp.dot(inputs, msg_weight, preferred_element_type=jnp.float32) + msg_bias).astype(jnp.bfloat16)
    node_ids = jnp.concatenate([source_id, target_id])
    summed = jax.ops.segment_sum(message.astype(jnp.float32), node_ids, num_segments=NODES)
    touched = jax.ops.segment_sum(jnp.ones(node_ids.shape, jnp.float32), node_ids, num_segments=NODES)
    mean_msg = (summed / jnp.maximum(touched, 1.0)[:, None]).astype(jnp.bfloat16)

    def node_block(pieces):
        block_msg, block_mem, block_touch = pieces
        fresh = gru_cell(block_msg, block_mem, input_weight, state_weight, input_bias, state_bias)
        return jnp.where(block_touch[:, None] > 0, fresh, block_mem)
    new_memory = lax.map(node_block, (mean_msg.reshape(DEVICES, NODE_DEV, M), memory.reshape(DEVICES, NODE_DEV, M), touched.reshape(DEVICES, NODE_DEV))).reshape(NODES, M)
    owner_dev = jnp.arange(QUERIES, dtype=jnp.int32) // Q_DEV
    features0 = new_memory[(owner_dev * NODE_DEV + query_rows).astype(jnp.int32)].astype(jnp.bfloat16)
    link_dev = jnp.arange(QUERIES * NB, dtype=jnp.int32) // (Q_DEV * NB)
    link_index = ((link_dev // N_MEMBER * N_MEMBER + link_member[:, 0]) * Q_DEV + link_slot).astype(jnp.int32)
    delta_code = time_code(link_delta, frequency, time_phase).reshape(QUERIES, NB, TD)
    self_code = time_code(jnp.zeros((QUERIES,), jnp.int32), frequency, time_phase)
    features1 = attend(features0, features0[link_index].reshape(QUERIES, NB, M), delta_code, self_code, query_weight[0], key_weight[0], value_weight[0], merge_weight[0], merge_bias[0], HEADS)
    embedding = attend(features1, features1[link_index].reshape(QUERIES, NB, M), delta_code, self_code, query_weight[1], key_weight[1], value_weight[1], merge_weight[1], merge_bias[1], HEADS)
    return (new_memory, embedding)
```

```python
import functools
import math

import jax
import jax.numpy as jnp
from jax import lax
from jax.experimental import pallas as pl
from jax.experimental.pallas import tpu as pltpu
from jax.sharding import PartitionSpec as P

MESH = pl.DeviceIdType.MESH
F32 = jnp.float32
BF16 = jnp.bfloat16
I32 = jnp.int32
HEADS = 2
FAN = 10
LANES = 128
NEG = -1e30


def iota(shape, dim):
    return lax.broadcasted_iota(I32, shape, dim)


def dot(a, b):
    return jnp.dot(a, b, preferred_element_type=F32)


def dot_t(a, b):
    return lax.dot_general(a, b, (((1,), (1,)), ((), ())), preferred_element_type=F32)


def cosine(x):
    turns = jnp.floor(x * (0.5 / math.pi) + 0.5)
    y = 0.5 * ((x - turns * 6.28125) - turns * (2.0 * math.pi - 6.28125))
    s = y * y
    p = 1.0 / 362880 - s * (1.0 / 39916800)
    p = -1.0 / 5040 + s * p
    p = 1.0 / 120 + s * p
    p = -1.0 / 6 + s * p
    sine = y + y * s * p
    return 1.0 - 2.0 * sine * sine


def column(row):
    n = row.shape[1]
    return jnp.sum(jnp.where(iota((n, n), 0) == iota((n, n), 1), row, 0.0), axis=1, keepdims=True)


def kernel(
    group_size,
    device_count,
    memory,
    s_owner,
    t_owner,
    s_row,
    t_row,
    e_time,
    q_rows,
    l_member,
    l_slot,
    l_delta,
    freq,
    phase,
    msg_w,
    msg_b,
    in_w,
    st_w,
    in_b,
    st_b,
    q_w,
    k_w,
    v_w,
    m_w,
    m_b,
    new_memory,
    embedding,
    mem,
    mem_hi,
    mem_lo,
    msg_v,
    in_v,
    st_v,
    q_v,
    k_v,
    v_v,
    m_v,
    req_out,
    req_in,
    slot_row,
    xout,
    fetched,
    yout,
    inbound,
    pick,
    place,
    msgs,
    back,
    touched,
    state,
    table,
    inverse,
    code,
    u_buf,
    cp,
    s_acc,
    acc,
    local_sem,
    out_sem,
    send_sem,
    recv_sem,
    hop_send,
    hop_recv,
):
    group = lax.axis_index("group")
    member = lax.axis_index("member")
    me = group * group_size + member
    nodes, width = mem.shape
    events = s_row.shape[1]
    queries = q_rows.shape[1]
    slots = device_count * 8
    barrier = pltpu.get_barrier_semaphore()

    def device(t):
        d = lax.rem(me + t, device_count)
        return d, {"group": lax.div(d, group_size), "member": lax.rem(d, group_size)}

    loads = [
        pltpu.make_async_copy(src, dst, local_sem.at[i])
        for i, (src, dst) in enumerate(
            [
                (memory, mem),
                (msg_w, msg_v),
                (st_w, st_v),
                (in_w, in_v),
                (q_w, q_v),
                (k_w, k_v),
                (v_w, v_v),
                (m_w, m_v),
            ]
        )
    ]
    for load in loads:
        load.start()

    def greet(t, _):
        _, dev = device(t + 1)
        pl.semaphore_signal(barrier, inc=1, device_id=dev, device_id_type=MESH)
        return 0

    lax.fori_loop(0, device_count - 1, greet, 0)

    places_row, places_col = [], []
    for role, owner_ref in enumerate((s_owner, t_owner)):
        own_row = owner_ref[...].astype(F32)
        own_col = column(own_row)
        same = own_col == own_row
        up = iota((events, events), 0) < iota((events, events), 1)
        down = iota((events, events), 1) < iota((events, events), 0)
        rank_row = jnp.sum(jnp.where(same & up, 1.0, 0.0), axis=0, keepdims=True)
        rank_col = jnp.sum(jnp.where(same & down, 1.0, 0.0), axis=1, keepdims=True)
        places_row.append(own_row * 8.0 + (rank_row + 4.0 * role))
        places_col.append(own_col * 8.0 + (rank_col + 4.0 * role))
    place_row = jnp.concatenate(places_row, axis=1).astype(I32)
    wanted_row = jnp.concatenate([s_row[...], t_row[...]], axis=1).astype(F32) + 1.0

    def request(j, _):
        base = j * LANES
        hit = place_row == iota((LANES, 2 * events), 0) + base
        asked = jnp.sum(jnp.where(hit, wanted_row, 0.0), axis=1, keepdims=True) - 1.0
        asked = jnp.broadcast_to(asked, (LANES, LANES)).astype(I32)
        req_out[pl.ds(j * 16, 16)] = asked.reshape(16, 8, LANES)
        return 0

    lax.fori_loop(0, slots // LANES, request, 0)

    pl.semaphore_wait(barrier, device_count - 1)

    def exchange_one(src, dst, t, sem):
        d, dev = device(t)
        pltpu.make_async_remote_copy(
            src_ref=src.at[d],
            dst_ref=dst.at[me],
            send_sem=send_sem.at[sem],
            recv_sem=recv_sem.at[sem],
            device_id=dev,
            device_id_type=MESH,
        ).start()

    def exchange_wait(src, dst, sem):
        part = dst.at[pl.ds(0, device_count - 1)]
        pltpu.make_async_copy(part, part, recv_sem.at[sem]).wait()
        part = src.at[pl.ds(0, device_count - 1)]
        pltpu.make_async_copy(part, part, send_sem.at[sem]).wait()

    def send_request(t, _):
        exchange_one(req_out, req_in, t + 1, 0)
        return 0

    lax.fori_loop(0, device_count - 1, send_request, 0)
    req_in[me] = req_out[me]

    loads[0].wait()

    def split(j, _):
        rows = pl.ds(j * LANES, LANES)
        x = mem[rows, :]
        hi = x.astype(BF16)
        mem_hi[rows, :] = hi
        mem_lo[rows, :] = (x - hi.astype(F32)).astype(BF16)
        return 0

    lax.fori_loop(0, nodes // LANES, split, 0)

    exchange_wait(req_out, req_in, 0)

    chunk = 2 * LANES
    peers = chunk // 8

    def chunk_of(j):
        return lax.rem(lax.div(me, peers) + j, device_count // peers)

    def send_chunk(src, dst, j, sem):
        first = chunk_of(j) * peers

        def one(i, _):
            d = first + lax.rem(lax.rem(me, peers) + i, peers)

            @pl.when(d != me)
            def _():
                exchange_one(src, dst, d - me + device_count, sem)

            return 0

        lax.fori_loop(0, peers, one, 0)

    def serve(j, _):
        c = chunk_of(j)
        asked = req_in[pl.ds(c * peers, peers)].reshape(chunk, LANES)
        lane = iota((chunk, LANES), 1)
        hot = [
            jnp.where(asked == lane + b * LANES, 1.0, 0.0).astype(BF16)
            for b in range(nodes // LANES)
        ]
        rows = dot(jnp.concatenate(hot, axis=1), mem_hi[...])
        xout[pl.ds(c * peers, peers)] = rows.reshape(peers, 8, width).astype(BF16)
        send_chunk(xout, fetched, j, 1)
        return 0

    lax.fori_loop(0, slots // chunk, serve, 0)
    fetched[me] = xout[me]

    lane_slots = iota((events, slots), 1)
    for role in range(2):
        hit = lane_slots == places_col[role].astype(I32)
        pick[pl.ds(role * events, events), :] = jnp.where(hit, 1.0, 0.0).astype(BF16)

    def placing(j, _):
        hit = place_row == iota((LANES, 2 * events), 0) + j * LANES
        place[pl.ds(j * LANES, LANES), :] = jnp.where(hit, 1.0, 0.0).astype(BF16)
        return 0

    lax.fori_loop(0, slots // LANES, placing, 0)

    time_col = column(e_time[...].astype(F32))
    stamp = cosine(time_col * freq[...] + phase[...]).astype(BF16)
    for load in loads[1:]:
        load.wait()
    stamped = dot(stamp, msg_v[pl.ds(2 * width, LANES), :]) + msg_b[...]

    for b in range(slots // LANES):
        asked = req_in[pl.ds(b * 16, 16)].reshape(LANES, LANES)
        diagonal = iota((LANES, LANES), 0) == iota((LANES, LANES), 1)
        slot_row[:, pl.ds(b * LANES, LANES)] = jnp.sum(
            jnp.where(diagonal, asked.astype(F32), 0.0), axis=0, keepdims=True
        )

    def back_matrix(j, _):
        rows = pl.ds(j * LANES, LANES)
        node = (iota((LANES, slots), 0) + j * LANES).astype(F32)
        hot = jnp.where(slot_row[...] == node, 1.0, 0.0)
        back[rows, :] = hot.astype(BF16)
        touched[rows, :] = jnp.broadcast_to(
            jnp.sum(hot, axis=1, keepdims=True), (LANES, LANES)
        )
        return 0

    lax.fori_loop(0, nodes // LANES, back_matrix, 0)

    exchange_wait(xout, fetched, 1)

    rows_in = fetched[...].reshape(slots, width)
    for role in range(2):
        msgs[pl.ds(role * events, events), :] = dot(
            pick[pl.ds(role * events, events), :], rows_in
        ).astype(BF16)
    source_mem = msgs[pl.ds(0, events), :]
    target_mem = msgs[pl.ds(events, events), :]
    first_w = msg_v[pl.ds(0, width), :]
    second_w = msg_v[pl.ds(width, width), :]
    to_source = dot(source_mem, first_w) + dot(target_mem, second_w) + stamped
    to_target = dot(target_mem, first_w) + dot(source_mem, second_w) + stamped
    msgs[pl.ds(0, events), :] = jnp.maximum(to_source, 0.0).astype(BF16)
    msgs[pl.ds(events, events), :] = jnp.maximum(to_target, 0.0).astype(BF16)

    def give_back(j, _):
        c = chunk_of(j)
        rows = dot(place[pl.ds(c * chunk, chunk), :], msgs[...])
        yout[pl.ds(c * peers, peers)] = rows.reshape(peers, 8, width).astype(BF16)
        send_chunk(yout, inbound, j, 2)
        return 0

    lax.fori_loop(0, slots // chunk, give_back, 0)
    inbound[me] = yout[me]

    query_col = column(q_rows[...].astype(F32))
    query_hot = jnp.where(
        iota((queries, nodes), 1).astype(F32) == query_col, 1.0, 0.0
    ).astype(BF16)
    query_slots = jnp.where(slot_row[...] == query_col, 1.0, 0.0)
    query_touched = jnp.sum(query_slots, axis=1, keepdims=True)
    query_slots = query_slots.astype(BF16)
    query_hi = dot(query_hot, mem_hi[...])
    query_mem = query_hi + dot(query_hot, mem_lo[...])
    query_state = dot(query_hi.astype(BF16), st_v[...]) + st_b[...]

    links = l_slot.shape[1]
    link_id = iota((queries, links), 1)
    first_link = iota((queries, links), 0) * FAN
    mine = (link_id >= first_link) & (link_id < first_link + FAN)
    link_f = iota((links, LANES), 0).astype(F32)
    link_k = link_f - FAN * jnp.floor((link_f + 0.5) * (1.0 / FAN))
    spread = jnp.where(link_k == iota((links, LANES), 1).astype(F32), 1.0, 0.0).astype(BF16)

    def arranged(row):
        return dot(jnp.where(mine, row.astype(F32), 0.0).astype(BF16), spread)

    lane_q = iota((queries, LANES), 1)
    live = lane_q < FAN
    slot_f = arranged(l_slot[...])
    member_f = arranged(l_member[...])
    high = jnp.right_shift(l_delta[...], 4)
    delta_f = arranged(high) * 16.0 + arranged(l_delta[...] - high * 16)
    slot_i = jnp.where(live, slot_f, 0.0).astype(I32)
    member_i = jnp.where(live, member_f, -1.0).astype(I32)
    link_i = member_i * LANES + slot_i

    for k in range(FAN):
        code[k] = cosine(delta_f[:, k : k + 1] * freq[...] + phase[...]).astype(BF16)
    self_code = cosine(phase[...]).astype(BF16)

    def invert(b, _):
        node = lane_q + b * LANES
        found = jnp.full((queries, LANES), LANES - 1, I32)
        for k in range(FAN):
            found = jnp.where(link_i[:, k : k + 1] == node, k, found)
        inverse[b] = found
        return 0

    lax.fori_loop(0, group_size, invert, 0)

    def states(j, _):
        rows = pl.ds(j * chunk, chunk)
        state[rows, :] = dot(mem_hi[rows, :], st_v[...]) + st_b[...]
        return 0

    lax.fori_loop(0, nodes // chunk, states, 0)

    exchange_wait(yout, inbound, 2)

    def cell(mean_msg, old, from_state):
        def part(i):
            return dot(mean_msg, in_v[:, i * width : (i + 1) * width]) + in_b[:, i * width : (i + 1) * width]

        reset = jax.nn.sigmoid(part(0) + from_state[:, :width])
        update = jax.nn.sigmoid(part(1) + from_state[:, width : 2 * width])
        candidate = jnp.tanh(part(2) + reset * from_state[:, 2 * width :])
        return (1.0 - update) * candidate + update * old

    messages_in = inbound[...].reshape(slots, width)
    query_mean = (dot(query_slots, messages_in) / jnp.maximum(query_touched, 1.0)).astype(BF16)
    fresh = cell(query_mean, query_mem, query_state)
    feats = jnp.where(query_touched > 0.0, fresh, query_mem).astype(BF16)

    def refresh(j, _):
        rows = pl.ds(j * LANES, LANES)
        count = touched[rows, 0:1]
        mean = dot(back[rows, :], inbound[...].reshape(slots, width)) / jnp.maximum(count, 1.0)
        old = mem[rows, :]
        new = cell(mean.astype(BF16), old, state[rows, :])
        mem[rows, :] = jnp.where(count > 0.0, new, old)
        return 0

    parity = lax.rem(member, 2)
    first_stride = 2 + 6 * parity
    second_stride = 8 - 6 * parity
    a_pos = lax.rem(lax.div(member, first_stride), 4)
    b_pos = lax.rem(lax.div(member, second_stride), 4)

    def at(da, db):
        return (
            lax.rem(a_pos + da + 4, 4) * first_stride
            + lax.rem(b_pos + db + 4, 4) * second_stride
            + parity
        )

    sibling = member + 1 - 2 * parity
    half = queries // 2

    for hop in range(2):
        rows_of = table.at[hop]
        sends = hop_send.at[hop]
        arrivals = hop_recv.at[hop]

        def piece(ref, which):
            return ref if which is None else ref.at[pl.ds(which * half, half)]

        def send(block, to, which=None):
            part = piece(rows_of.at[block], which)
            pltpu.make_async_remote_copy(
                src_ref=part,
                dst_ref=part,
                send_sem=sends,
                recv_sem=arrivals.at[block, 1 if which == 1 else 0],
                device_id={"member": to},
                device_id_type=MESH,
            ).start()

        def arrive(block, which=None):
            part = piece(rows_of.at[block], which)
            pltpu.make_async_copy(part, part, arrivals.at[block, 1 if which == 1 else 0]).wait()

        a_next, a_last, b_next, b_last = at(1, 0), at(-1, 0), at(0, 1), at(0, -1)

        rows_of[member] = feats
        for to in (a_next, a_last, b_next, b_last, sibling):
            send(member, to)

        query_w = q_v.at[hop]
        key_w = k_v.at[hop]
        merge_w = m_v.at[hop]
        query_vec = dot(feats, query_w[pl.ds(0, width), :]) + dot(
            jnp.broadcast_to(self_code, (8, LANES)), query_w[pl.ds(width, LANES), :]
        )[0:1]
        merged_self = dot(feats, merge_w[pl.ds(width, width), :]) + m_b[hop : hop + 1, :]
        head = width // HEADS
        for h in range(HEADS):
            u = dot_t(
                (query_vec[:, h * head : (h + 1) * head] * (1.0 / math.sqrt(head))).astype(BF16),
                key_w[:, h * head : (h + 1) * head],
            )
            u_buf[pl.ds(h * queries, queries), :] = u[:, :width].astype(BF16)
            u_code = u[:, width:]
            c = jnp.full((queries, LANES), NEG, F32)
            for k in range(FAN):
                c = jnp.where(
                    lane_q == k,
                    jnp.sum(u_code * code[k].astype(F32), axis=1, keepdims=True),
                    c,
                )
            most = c
            for k in range(FAN):
                alike = (link_i == link_i[:, k : k + 1]) & live
                most = jnp.where(alike, jnp.maximum(most, c[:, k : k + 1]), most)
            total = jnp.zeros((queries, LANES), F32)
            for k in range(FAN):
                alike = (link_i == link_i[:, k : k + 1]) & live
                total = total + jnp.where(alike, jnp.exp(c[:, k : k + 1] - most), 0.0)
            cp[h] = jnp.where(live, most + jnp.log(jnp.where(live, total, 1.0)), NEG)
            cp[HEADS + h] = c
            s_acc[h] = jnp.zeros((queries, LANES), F32)
        acc[...] = jnp.zeros_like(acc)

        def attend(da, db):
            chip = lax.div(at(da, db), 2)
            arrive(2 * chip + 1 - parity)
            rows = rows_of[pl.ds(2 * chip, 2)].reshape(2 * queries, width)
            scores = dot_t(u_buf[...], rows)
            parts = []
            for h in range(HEADS):
                sides = []
                for side in range(2):
                    s = scores[
                        h * queries : (h + 1) * queries, side * queries : (side + 1) * queries
                    ]
                    bias = jnp.take_along_axis(cp[h], inverse[2 * chip + side], axis=1)
                    sides.append(jnp.exp(s + bias).astype(BF16))
                    picked = jnp.take_along_axis(s, slot_i, axis=1)
                    s_acc[h] = jnp.where(member_i == 2 * chip + side, picked, s_acc[h])
                parts.append(jnp.concatenate(sides, axis=1))
            acc[...] += dot(jnp.concatenate(parts, axis=0), rows)

        if hop == 0:
            lax.fori_loop(0, 4, refresh, 0)

        arrive(at(-1, 0))
        send(at(-1, 0), a_next, 0)
        for to in (b_next, b_last, sibling):
            send(at(-1, 0), to)
        arrive(at(1, 0))
        send(at(1, 0), a_last, 1)
        for to in (b_next, b_last, sibling):
            send(at(1, 0), to)
        arrive(at(0, -1))
        send(at(0, -1), b_next, 0)
        send(at(0, -1), sibling)
        arrive(at(0, 1))
        send(at(0, 1), b_last, 1)
        send(at(0, 1), sibling)
        attend(0, 0)
        for which in range(2):
            arrive(at(2, 0), which)
        for to in (b_next, b_last, sibling):
            send(at(2, 0), to)
        for which in range(2):
            arrive(at(0, 2), which)
        send(at(0, 2), sibling)
        if hop == 0:
            lax.fori_loop(4, 8, refresh, 0)
        for da, db in ((-1, 0), (1, 0), (0, -1), (0, 1)):
            attend(da, db)
        for da in (-1, 1):
            for db in (-1, 1):
                arrive(at(da, db))
                send(at(da, db), b_next if db == -1 else b_last, 0 if db == -1 else 1)
                send(at(da, db), sibling)
        attend(2, 0)
        attend(0, 2)
        for db in (-1, 1):
            arrive(at(2, db))
            send(at(2, db), b_next if db == -1 else b_last, 0 if db == -1 else 1)
            send(at(2, db), sibling)
        for da in (-1, 1):
            for which in range(2):
                arrive(at(da, 2), which)
            send(at(da, 2), sibling)
        for da in (-1, 1):
            for db in (-1, 1):
                attend(da, db)
        for which in range(2):
            arrive(at(2, 2), which)
        send(at(2, 2), sibling)
        for da, db in ((2, -1), (2, 1), (-1, 2), (1, 2)):
            attend(da, db)
        if hop == 0:
            store = pltpu.make_async_copy(mem, new_memory, out_sem)
            store.start()
        attend(2, 2)

        value_w = v_v.at[hop]
        mixed = []
        for h in range(HEADS):
            w = jnp.where(live, jnp.exp(s_acc[h] + cp[HEADS + h]), 0.0)
            scale = 1.0 / jnp.sum(w, axis=1, keepdims=True)
            w = w * scale
            coded = jnp.zeros((queries, LANES), F32)
            for k in range(FAN):
                coded = coded + w[:, k : k + 1] * code[k].astype(F32)
            rows = (acc[pl.ds(h * queries, queries), :] * scale).astype(BF16)
            cols = slice(h * head, (h + 1) * head)
            mixed.append(
                dot(rows, value_w[pl.ds(0, width), cols])
                + dot(coded.astype(BF16), value_w[pl.ds(width, LANES), cols])
            )
        mixed = jnp.concatenate(mixed, axis=1).astype(BF16)
        merged = dot(mixed, merge_w[pl.ds(0, width), :]) + merged_self
        feats = jnp.maximum(merged, 0.0).astype(BF16)

        whole = rows_of.at[pl.ds(0, group_size - 1)]
        pltpu.make_async_copy(whole, whole, sends).wait()

    embedding[...] = feats
    store.wait()


def on_device(
    memory,
    source_owner,
    target_owner,
    source_row,
    target_row,
    event_time,
    query_rows,
    link_member,
    link_slot,
    link_delta,
    frequency,
    time_phase,
    msg_weight,
    msg_bias,
    input_weight,
    state_weight,
    input_bias,
    state_bias,
    query_weight,
    key_weight,
    value_weight,
    merge_weight,
    merge_bias,
):
    device_count = lax.axis_size(("group", "member"))
    group_size = lax.axis_size("member")
    nodes, width = memory.shape
    events = source_row.shape[0]
    queries = query_rows.shape[0]
    slots = device_count * 8

    def flat(x):
        return x.reshape(1, -1)

    vmem = pl.BlockSpec(memory_space=pltpu.VMEM)
    hbm = pl.BlockSpec(memory_space=pl.ANY)
    return pl.pallas_call(
        functools.partial(kernel, group_size, device_count),
        out_shape=(
            jax.ShapeDtypeStruct((nodes, width), F32),
            jax.ShapeDtypeStruct((queries, width), BF16),
        ),
        in_specs=[hbm] + [vmem] * 11 + [hbm, vmem, hbm, hbm, vmem, vmem] + [hbm] * 4 + [vmem],
        out_specs=(hbm, vmem),
        scratch_shapes=[
            pltpu.VMEM((nodes, width), F32),
            pltpu.VMEM((nodes, width), BF16),
            pltpu.VMEM((nodes, width), BF16),
            pltpu.VMEM(msg_weight.shape, BF16),
            pltpu.VMEM(input_weight.shape, BF16),
            pltpu.VMEM(state_weight.shape, BF16),
            pltpu.VMEM(query_weight.shape, BF16),
            pltpu.VMEM(key_weight.shape, BF16),
            pltpu.VMEM(value_weight.shape, BF16),
            pltpu.VMEM(merge_weight.shape, BF16),
            pltpu.VMEM((device_count, 8, LANES), I32),
            pltpu.VMEM((device_count, 8, LANES), I32),
            pltpu.VMEM((1, slots), F32),
            pltpu.VMEM((device_count, 8, width), BF16),
            pltpu.VMEM((device_count, 8, width), BF16),
            pltpu.VMEM((device_count, 8, width), BF16),
            pltpu.VMEM((device_count, 8, width), BF16),
            pltpu.VMEM((2 * events, slots), BF16),
            pltpu.VMEM((slots, 2 * events), BF16),
            pltpu.VMEM((2 * events, width), BF16),
            pltpu.VMEM((nodes, slots), BF16),
            pltpu.VMEM((nodes, LANES), F32),
            pltpu.VMEM((nodes, 3 * width), F32),
            pltpu.VMEM((2, group_size, queries, width), BF16),
            pltpu.VMEM((group_size, queries, LANES), I32),
            pltpu.VMEM((FAN, queries, LANES), BF16),
            pltpu.VMEM((HEADS * queries, width), BF16),
            pltpu.VMEM((2 * HEADS, queries, LANES), F32),
            pltpu.VMEM((HEADS, queries, LANES), F32),
            pltpu.VMEM((HEADS * queries, width), F32),
            pltpu.SemaphoreType.DMA((8,)),
            pltpu.SemaphoreType.DMA,
            pltpu.SemaphoreType.DMA((3,)),
            pltpu.SemaphoreType.DMA((3,)),
            pltpu.SemaphoreType.DMA((2,)),
            pltpu.SemaphoreType.DMA((2, group_size, 2)),
        ],
        compiler_params=pltpu.CompilerParams(
            collective_id=0, has_side_effects=True, vmem_limit_bytes=56 * 2**20
        ),
    )(
        memory,
        flat(source_owner),
        flat(target_owner),
        flat(source_row),
        flat(target_row),
        flat(event_time),
        flat(query_rows),
        flat(link_member),
        flat(link_slot),
        flat(link_delta),
        flat(frequency),
        flat(time_phase),
        msg_weight,
        flat(msg_bias),
        input_weight,
        state_weight,
        flat(input_bias),
        flat(state_bias),
        query_weight,
        key_weight,
        value_weight,
        merge_weight,
        merge_bias,
    )


def solution(mesh):
    both = ("group", "member")
    rows = P(both, None)
    flat = P(both)
    in_specs = (rows,) * 3 + (flat,) * 4 + (rows,) + (flat,) * 2 + (P(),) * 13
    return jax.shard_map(
        on_device, mesh=mesh, in_specs=in_specs, out_specs=(rows, rows), check_vma=False
    )
```

```python
import functools
import math

import jax
import jax.numpy as jnp
from jax import lax
from jax.experimental import pallas as pl
from jax.experimental.pallas import tpu as pltpu
from jax.sharding import PartitionSpec as P

MESH = pl.DeviceIdType.MESH
F32 = jnp.float32
BF16 = jnp.bfloat16
I32 = jnp.int32
HEADS = 2
FAN = 10
LANES = 128
NEG = -1e30


def iota(shape, dim):
    return lax.broadcasted_iota(I32, shape, dim)


def dot(a, b):
    return jnp.dot(a, b, preferred_element_type=F32)


def dot_t(a, b):
    return lax.dot_general(a, b, (((1,), (1,)), ((), ())), preferred_element_type=F32)


def cosine(x):
    turns = jnp.floor(x * (0.5 / math.pi) + 0.5)
    y = 0.5 * ((x - turns * 6.28125) - turns * (2.0 * math.pi - 6.28125))
    s = y * y
    p = 1.0 / 362880 - s * (1.0 / 39916800)
    p = -1.0 / 5040 + s * p
    p = 1.0 / 120 + s * p
    p = -1.0 / 6 + s * p
    sine = y + y * s * p
    return 1.0 - 2.0 * sine * sine


def column(row):
    n = row.shape[1]
    return jnp.sum(jnp.where(iota((n, n), 0) == iota((n, n), 1), row, 0.0), axis=1, keepdims=True)


def lanes_row(ref):
    return jnp.concatenate([ref[i : i + 1, :] for i in range(ref.shape[0])], axis=1)


def kernel(
    group_size,
    device_count,
    memory,
    s_owner,
    t_owner,
    s_row,
    t_row,
    e_time,
    q_rows,
    l_member,
    l_slot,
    l_delta,
    freq,
    phase,
    msg_w,
    msg_b,
    in_w,
    st_w,
    in_b,
    st_b,
    q_w,
    k_w,
    v_w,
    m_w,
    m_b,
    new_memory,
    embedding,
    mem_hi,
    mem_lo,
    msg_v,
    in_v,
    st_v,
    q_v,
    k_v,
    v_v,
    m_v,
    req_out,
    req_in,
    req_rows,
    slot_row,
    xout,
    fetched,
    yout,
    inbound,
    pick,
    place,
    msgs,
    back,
    touched,
    state,
    table,
    inverse,
    code,
    u_buf,
    cp,
    s_acc,
    acc,
    local_sem,
    out_sem,
    send_sem,
    recv_sem,
    hop_send,
    hop_recv,
):
    mem = new_memory
    group = lax.axis_index("group")
    member = lax.axis_index("member")
    me = group * group_size + member
    nodes, width = mem.shape
    in_bias = lanes_row(in_b)
    st_bias = lanes_row(st_b)
    events = s_row.shape[1]
    queries = q_rows.shape[1]
    slots = device_count * 8
    barrier = pltpu.get_barrier_semaphore()

    x_pos = lax.rem(lax.div(member, 2), 4)
    z_pos = lax.div(member, 8)
    core = lax.rem(member, 2)
    batch = lax.rem(group + z_pos + x_pos, 4)
    place_me = batch * 32 + group * 8 + z_pos * 2 + core

    def position(owner):
        y = jnp.right_shift(owner, 5)
        z = jnp.bitwise_and(jnp.right_shift(owner, 3), 3)
        x = jnp.bitwise_and(jnp.right_shift(owner, 1), 3)
        return jnp.bitwise_and(x + y + z, 3) * 32 + y * 8 + z * 2 + jnp.bitwise_and(owner, 1)

    def device(t):
        d = lax.rem(me + t, device_count)
        return d, {"group": lax.div(d, group_size), "member": lax.rem(d, group_size)}

    loads = [
        pltpu.make_async_copy(src, dst, local_sem.at[i])
        for i, (src, dst) in enumerate(
            [
                (memory, mem),
                (msg_w, msg_v),
                (st_w, st_v),
                (in_w, in_v),
                (q_w, q_v),
                (k_w, k_v),
                (v_w, v_v),
                (m_w, m_v),
            ]
        )
    ]
    for load in loads:
        load.start()

    def greet(t, _):
        _, dev = device(t + 1)
        pl.semaphore_signal(barrier, inc=1, device_id=dev, device_id_type=MESH)
        return 0

    lax.fori_loop(0, device_count - 1, greet, 0)

    places_row, places_col = [], []
    for role, owner_ref in enumerate((s_owner, t_owner)):
        own_row = position(owner_ref[...]).astype(F32)
        own_col = column(own_row)
        same = own_col == own_row
        up = iota((events, events), 0) < iota((events, events), 1)
        down = iota((events, events), 1) < iota((events, events), 0)
        rank_row = jnp.sum(jnp.where(same & up, 1.0, 0.0), axis=0, keepdims=True)
        rank_col = jnp.sum(jnp.where(same & down, 1.0, 0.0), axis=1, keepdims=True)
        places_row.append(own_row * 8.0 + (rank_row + 4.0 * role))
        places_col.append(own_col * 8.0 + (rank_col + 4.0 * role))
    place_row = jnp.concatenate(places_row, axis=1).astype(I32)
    wanted_row = jnp.concatenate([s_row[...], t_row[...]], axis=1).astype(F32) + 1.0

    lane_d = iota((device_count, LANES), 1)
    asked_out = jnp.zeros((device_count, LANES), F32)
    for slot in range(8):
        role_lanes = slice(0, events) if slot < 4 else slice(events, 2 * events)
        hit = place_row[:, role_lanes] == iota((device_count, events), 0) * 8 + slot
        asked = jnp.sum(jnp.where(hit, wanted_row[:, role_lanes], 0.0), axis=1, keepdims=True)
        asked_out = jnp.where(lane_d == slot, asked - 1.0, asked_out)
    req_out[:, 0, :] = asked_out.astype(I32)

    pl.semaphore_wait(barrier, device_count - 1)

    def exchange(src, dst, j, sem):
        def one(i, _):
            q = lax.rem(lax.rem(i, 16) * 7, 16)
            y = lax.rem(group + lax.div(q, 4), 4)
            z = lax.rem(z_pos + lax.rem(q, 4), 4)
            c = lax.rem(core + i + lax.div(i, 16), 2)
            k = lax.rem(batch + j, 4)
            x = lax.rem(k - y - z + 8, 4)
            place = k * 32 + y * 8 + z * 2 + c

            @pl.when(place != place_me)
            def _():
                pltpu.make_async_remote_copy(
                    src_ref=src.at[place],
                    dst_ref=dst.at[place_me],
                    send_sem=send_sem.at[sem],
                    recv_sem=recv_sem.at[sem],
                    device_id={"group": y, "member": z * 8 + x * 2 + c},
                    device_id_type=MESH,
                ).start()

            return 0

        lax.fori_loop(0, 32, one, 0)

    def exchange_wait(src, dst, sem):
        part = dst.at[pl.ds(0, device_count - 1)]
        pltpu.make_async_copy(part, part, recv_sem.at[sem]).wait()
        part = src.at[pl.ds(0, device_count - 1)]
        pltpu.make_async_copy(part, part, send_sem.at[sem]).wait()

    def send_requests(j, _):
        exchange(req_out, req_in, j + 1, 0)
        return 0

    lax.fori_loop(0, 4, send_requests, 0)
    req_in[place_me] = req_out[place_me]

    loads[0].wait()

    def split(j, _):
        rows = pl.ds(j * LANES, LANES)
        x = mem[rows, :]
        hi = x.astype(BF16)
        mem_hi[rows, :] = hi
        mem_lo[rows, :] = (x - hi.astype(F32)).astype(BF16)
        return 0

    lax.fori_loop(0, nodes // LANES, split, 0)

    exchange_wait(req_out, req_in, 0)

    chunk = 2 * LANES
    peers = chunk // 8
    req_rows[...] = req_in[:, 0, :]

    def asked_column(first, count):
        part = req_rows[pl.ds(first, count), :].astype(F32)
        spread_out = jnp.broadcast_to(part[:, None, :], (count, 8, LANES))
        mine_of = iota((count, 8, LANES), 1) == iota((count, 8, LANES), 2)
        column_of = jnp.sum(jnp.where(mine_of, spread_out, 0.0), axis=2, keepdims=True)
        return column_of.reshape(count * 8, 1)

    def serve(j, _):
        c = lax.rem(batch + j + 1, 4)
        asked = asked_column(pl.multiple_of(c * peers, peers), peers)
        lane = iota((chunk, LANES), 1).astype(F32)
        hot = [
            jnp.where(asked == lane + float(b * LANES), 1.0, 0.0).astype(BF16)
            for b in range(nodes // LANES)
        ]
        rows = dot(jnp.concatenate(hot, axis=1), mem_hi[...])
        xout[pl.ds(c * peers, peers)] = rows.reshape(peers, 8, width).astype(BF16)
        exchange(xout, fetched, j + 1, 1)
        return 0

    lax.fori_loop(0, slots // chunk, serve, 0)
    fetched[place_me] = xout[place_me]

    lane_slots = iota((events, slots), 1)
    for role in range(2):
        hit = lane_slots == places_col[role].astype(I32)
        pick[pl.ds(role * events, events), :] = jnp.where(hit, 1.0, 0.0).astype(BF16)

    def placing(j, _):
        hit = place_row == iota((LANES, 2 * events), 0) + j * LANES
        place[pl.ds(j * LANES, LANES), :] = jnp.where(hit, 1.0, 0.0).astype(BF16)
        return 0

    lax.fori_loop(0, slots // LANES, placing, 0)

    time_col = column(e_time[...].astype(F32))
    stamp = cosine(time_col * freq[...] + phase[...]).astype(BF16)
    for load in loads[1:]:
        load.wait()
    stamped = dot(stamp, msg_v[pl.ds(2 * width, LANES), :]) + msg_b[...]

    for b in range(slots // LANES):
        asked = asked_column(b * 16, 16)
        diagonal = iota((LANES, LANES), 0) == iota((LANES, LANES), 1)
        slot_row[:, pl.ds(b * LANES, LANES)] = jnp.sum(
            jnp.where(diagonal, asked, 0.0), axis=0, keepdims=True
        )

    def back_matrix(j, _):
        rows = pl.ds(j * LANES, LANES)
        node = (iota((LANES, slots), 0) + j * LANES).astype(F32)
        hot = jnp.where(slot_row[...] == node, 1.0, 0.0)
        back[rows, :] = hot.astype(BF16)
        touched[rows, :] = jnp.broadcast_to(
            jnp.sum(hot, axis=1, keepdims=True), (LANES, LANES)
        )
        return 0

    lax.fori_loop(0, nodes // LANES, back_matrix, 0)

    exchange_wait(xout, fetched, 1)

    rows_in = fetched[...].reshape(slots, width)
    for role in range(2):
        msgs[pl.ds(role * events, events), :] = dot(
            pick[pl.ds(role * events, events), :], rows_in
        ).astype(BF16)
    source_mem = msgs[pl.ds(0, events), :]
    target_mem = msgs[pl.ds(events, events), :]
    first_w = msg_v[pl.ds(0, width), :]
    second_w = msg_v[pl.ds(width, width), :]
    to_source = dot(source_mem, first_w) + dot(target_mem, second_w) + stamped
    to_target = dot(target_mem, first_w) + dot(source_mem, second_w) + stamped
    msgs[pl.ds(0, events), :] = jnp.maximum(to_source, 0.0).astype(BF16)
    msgs[pl.ds(events, events), :] = jnp.maximum(to_target, 0.0).astype(BF16)

    def give_back(j, _):
        c = lax.rem(batch + j + 1, 4)
        rows = dot(place[pl.ds(c * chunk, chunk), :], msgs[...])
        yout[pl.ds(c * peers, peers)] = rows.reshape(peers, 8, width).astype(BF16)
        exchange(yout, inbound, j + 1, 2)
        return 0

    lax.fori_loop(0, slots // chunk, give_back, 0)
    inbound[place_me] = yout[place_me]

    query_col = column(q_rows[...].astype(F32))
    query_hot = jnp.where(
        iota((queries, nodes), 1).astype(F32) == query_col, 1.0, 0.0
    ).astype(BF16)
    query_slots = jnp.where(slot_row[...] == query_col, 1.0, 0.0)
    query_touched = jnp.sum(query_slots, axis=1, keepdims=True)
    query_slots = query_slots.astype(BF16)
    query_hi = dot(query_hot, mem_hi[...])
    query_mem = query_hi + dot(query_hot, mem_lo[...])
    query_state = dot(query_hi.astype(BF16), st_v[...]) + st_bias

    slot_of = lanes_row(l_slot)
    delta_of = lanes_row(l_delta)
    member_of = l_member[...]
    links = slot_of.shape[1]
    link_id = iota((queries, links), 1)
    first_link = iota((queries, links), 0) * FAN
    mine = (link_id >= first_link) & (link_id < first_link + FAN)
    link_f = iota((links, LANES), 0).astype(F32)
    link_k = link_f - FAN * jnp.floor((link_f + 0.5) * (1.0 / FAN))
    spread = jnp.where(link_k == iota((links, LANES), 1).astype(F32), 1.0, 0.0).astype(BF16)

    def arranged(row):
        return dot(jnp.where(mine, row.astype(F32), 0.0).astype(BF16), spread)

    lane_q = iota((queries, LANES), 1)
    live = lane_q < FAN
    slot_f = arranged(slot_of)
    member_f = arranged(member_of)
    high = jnp.right_shift(delta_of, 4)
    delta_f = arranged(high) * 16.0 + arranged(delta_of - high * 16)
    slot_i = jnp.where(live, slot_f, 0.0).astype(I32)
    member_i = jnp.where(live, member_f, -1.0).astype(I32)
    link_i = member_i * LANES + slot_i

    for k in range(FAN):
        code[k] = cosine(delta_f[:, k : k + 1] * freq[...] + phase[...]).astype(BF16)
    self_code = cosine(phase[...]).astype(BF16)

    def invert(b, _):
        node = lane_q + b * LANES
        found = jnp.full((queries, LANES), LANES - 1, I32)
        for k in range(FAN):
            found = jnp.where(link_i[:, k : k + 1] == node, k, found)
        inverse[b] = found
        return 0

    lax.fori_loop(0, group_size, invert, 0)

    def states(j, _):
        rows = pl.ds(j * chunk, chunk)
        state[rows, :] = dot(mem_hi[rows, :], st_v[...]) + st_bias
        return 0

    lax.fori_loop(0, nodes // chunk, states, 0)

    exchange_wait(yout, inbound, 2)

    def cell(mean_msg, old, from_state):
        def part(i):
            return dot(mean_msg, in_v[:, i * width : (i + 1) * width]) + in_bias[:, i * width : (i + 1) * width]

        reset = jax.nn.sigmoid(part(0) + from_state[:, :width])
        update = jax.nn.sigmoid(part(1) + from_state[:, width : 2 * width])
        candidate = jnp.tanh(part(2) + reset * from_state[:, 2 * width :])
        return (1.0 - update) * candidate + update * old

    messages_in = inbound[...].reshape(slots, width)
    query_mean = (dot(query_slots, messages_in) / jnp.maximum(query_touched, 1.0)).astype(BF16)
    fresh = cell(query_mean, query_mem, query_state)
    feats = jnp.where(query_touched > 0.0, fresh, query_mem).astype(BF16)

    def refresh(j, _):
        rows = pl.ds(j * LANES, LANES)
        count = touched[rows, 0:1]
        mean = dot(back[rows, :], inbound[...].reshape(slots, width)) / jnp.maximum(count, 1.0)
        old = mem[rows, :]
        new = cell(mean.astype(BF16), old, state[rows, :])
        mem[rows, :] = jnp.where(count > 0.0, new, old)
        return 0

    parity = lax.rem(member, 2)
    first_stride = 2 + 6 * parity
    second_stride = 8 - 6 * parity
    a_pos = lax.rem(lax.div(member, first_stride), 4)
    b_pos = lax.rem(lax.div(member, second_stride), 4)

    def at(da, db):
        return (
            lax.rem(a_pos + da + 4, 4) * first_stride
            + lax.rem(b_pos + db + 4, 4) * second_stride
            + parity
        )

    sibling = member + 1 - 2 * parity
    half = queries // 2

    for hop in range(2):
        rows_of = table.at[hop]
        sends = hop_send.at[hop]
        arrivals = hop_recv.at[hop]

        def piece(ref, which):
            return ref if which is None else ref.at[pl.ds(which * half, half)]

        def send(block, to, which=None):
            part = piece(rows_of.at[block], which)
            pltpu.make_async_remote_copy(
                src_ref=part,
                dst_ref=part,
                send_sem=sends,
                recv_sem=arrivals.at[block, 1 if which == 1 else 0],
                device_id={"member": to},
                device_id_type=MESH,
            ).start()

        def arrive(block, which=None):
            part = piece(rows_of.at[block], which)
            pltpu.make_async_copy(part, part, arrivals.at[block, 1 if which == 1 else 0]).wait()

        a_next, a_last, b_next, b_last = at(1, 0), at(-1, 0), at(0, 1), at(0, -1)

        rows_of[member] = feats
        for to, which in ((a_next, 0), (a_last, 1), (a_next, 1), (a_last, 0)):
            send(member, to, which)
        send(member, b_next, 0)
        send(member, b_last, 1)
        send(member, sibling)
        send(member, b_next, 1)
        send(member, b_last, 0)

        query_w = q_v.at[hop]
        key_w = k_v.at[hop]
        merge_w = m_v.at[hop]
        query_vec = dot(feats, query_w[pl.ds(0, width), :]) + dot(
            jnp.broadcast_to(self_code, (8, LANES)), query_w[pl.ds(width, LANES), :]
        )[0:1]
        merged_self = dot(feats, merge_w[pl.ds(width, width), :]) + m_b[hop : hop + 1, :]
        head = width // HEADS
        for h in range(HEADS):
            u = dot_t(
                (query_vec[:, h * head : (h + 1) * head] * (1.0 / math.sqrt(head))).astype(BF16),
                key_w[:, h * head : (h + 1) * head],
            )
            u_buf[pl.ds(h * queries, queries), :] = u[:, :width].astype(BF16)
            u_code = u[:, width:]
            c = jnp.full((queries, LANES), NEG, F32)
            for k in range(FAN):
                c = jnp.where(
                    lane_q == k,
                    jnp.sum(u_code * code[k].astype(F32), axis=1, keepdims=True),
                    c,
                )
            most = c
            for k in range(FAN):
                alike = (link_i == link_i[:, k : k + 1]) & live
                most = jnp.where(alike, jnp.maximum(most, c[:, k : k + 1]), most)
            total = jnp.zeros((queries, LANES), F32)
            for k in range(FAN):
                alike = (link_i == link_i[:, k : k + 1]) & live
                total = total + jnp.where(alike, jnp.exp(c[:, k : k + 1] - most), 0.0)
            cp[h] = jnp.where(live, most + jnp.log(jnp.where(live, total, 1.0)), NEG)
            cp[HEADS + h] = c
            s_acc[h] = jnp.zeros((queries, LANES), F32)
        acc[...] = jnp.zeros_like(acc)

        def attend(da, db):
            chip = lax.div(at(da, db), 2)
            arrive(2 * chip + 1 - parity)
            rows = rows_of[pl.ds(2 * chip, 2)].reshape(2 * queries, width)
            scores = dot_t(u_buf[...], rows)
            parts = []
            for h in range(HEADS):
                sides = []
                for side in range(2):
                    s = scores[
                        h * queries : (h + 1) * queries, side * queries : (side + 1) * queries
                    ]
                    bias = jnp.take_along_axis(cp[h], inverse[2 * chip + side], axis=1)
                    sides.append(jnp.exp(s + bias).astype(BF16))
                    picked = jnp.take_along_axis(s, slot_i, axis=1)
                    s_acc[h] = jnp.where(member_i == 2 * chip + side, picked, s_acc[h])
                parts.append(jnp.concatenate(sides, axis=1))
            acc[...] += dot(jnp.concatenate(parts, axis=0), rows)

        lax.fori_loop(hop * 4, hop * 4 + 2, refresh, 0)
        near, far, across = at(-1, 0), at(1, 0), at(2, 0)
        arrive(near, 0)
        send(near, a_next, 0)
        send(near, b_next, 0)
        arrive(far, 1)
        send(far, a_last, 1)
        send(far, b_last, 1)
        arrive(near, 1)
        send(near, b_last, 1)
        send(near, b_next, 1)
        arrive(far, 0)
        send(far, b_next, 0)
        send(far, b_last, 0)
        send(near, b_last, 0)
        send(far, b_next, 1)
        arrive(at(0, -1), 0)
        send(at(0, -1), b_next, 0)
        arrive(at(0, 1), 1)
        send(at(0, 1), b_last, 1)
        send(near, sibling)
        send(far, sibling)
        lax.fori_loop(hop * 4 + 2, hop * 4 + 3, refresh, 0)
        attend(0, 0)
        arrive(across, 0)
        send(across, b_next, 0)
        arrive(across, 1)
        send(across, b_last, 1)
        send(across, b_next, 1)
        send(across, b_last, 0)
        send(across, sibling)
        arrive(at(0, -1), 1)
        send(at(0, -1), sibling)
        arrive(at(0, 1), 0)
        send(at(0, 1), sibling)
        lax.fori_loop(hop * 4 + 3, hop * 4 + 4, refresh, 0)
        if hop == 1:
            pass
        attend(-1, 0)
        for da in (-1, 1):
            arrive(at(da, -1), 0)
            send(at(da, -1), b_next, 0)
            arrive(at(da, 1), 1)
            send(at(da, 1), b_last, 1)
        attend(1, 0)
        attend(0, -1)
        for da in (-1, 1):
            arrive(at(da, -1), 1)
            send(at(da, -1), sibling)
            arrive(at(da, 1), 0)
            send(at(da, 1), sibling)
        arrive(at(2, -1), 0)
        send(at(2, -1), b_next, 0)
        arrive(at(2, 1), 1)
        send(at(2, 1), b_last, 1)
        attend(0, 1)
        for which in range(2):
            arrive(at(0, 2), which)
        send(at(0, 2), sibling)
        arrive(at(2, -1), 1)
        send(at(2, -1), sibling)
        arrive(at(2, 1), 0)
        send(at(2, 1), sibling)
        for da in (-1, 1):
            for db in (-1, 1):
                attend(da, db)
        for da in (-1, 1):
            for which in range(2):
                arrive(at(da, 2), which)
            send(at(da, 2), sibling)
        attend(2, 0)
        attend(0, 2)
        for which in range(2):
            arrive(at(2, 2), which)
        send(at(2, 2), sibling)
        for da, db in ((2, -1), (2, 1), (-1, 2), (1, 2), (2, 2)):
            attend(da, db)

        value_w = v_v.at[hop]
        mixed = []
        for h in range(HEADS):
            w = jnp.where(live, jnp.exp(s_acc[h] + cp[HEADS + h]), 0.0)
            scale = 1.0 / jnp.sum(w, axis=1, keepdims=True)
            w = w * scale
            coded = jnp.zeros((queries, LANES), F32)
            for k in range(FAN):
                coded = coded + w[:, k : k + 1] * code[k].astype(F32)
            rows = (acc[pl.ds(h * queries, queries), :] * scale).astype(BF16)
            cols = slice(h * head, (h + 1) * head)
            mixed.append(
                dot(rows, value_w[pl.ds(0, width), cols])
                + dot(coded.astype(BF16), value_w[pl.ds(width, LANES), cols])
            )
        mixed = jnp.concatenate(mixed, axis=1).astype(BF16)
        merged = dot(mixed, merge_w[pl.ds(0, width), :]) + merged_self
        feats = jnp.maximum(merged, 0.0).astype(BF16)

        whole = rows_of.at[pl.ds(0, group_size - 1)]
        pltpu.make_async_copy(whole, whole, sends).wait()

    embedding[...] = feats


def on_device(
    memory,
    source_owner,
    target_owner,
    source_row,
    target_row,
    event_time,
    query_rows,
    link_member,
    link_slot,
    link_delta,
    frequency,
    time_phase,
    msg_weight,
    msg_bias,
    input_weight,
    state_weight,
    input_bias,
    state_bias,
    query_weight,
    key_weight,
    value_weight,
    merge_weight,
    merge_bias,
):
    device_count = lax.axis_size(("group", "member"))
    group_size = lax.axis_size("member")
    nodes, width = memory.shape
    events = source_row.shape[0]
    queries = query_rows.shape[0]
    slots = device_count * 8

    def flat(x):
        return x.reshape(1, -1)

    def rows_of_lanes(x):
        return x.reshape(-1, LANES)

    vmem = pl.BlockSpec(memory_space=pltpu.VMEM)
    hbm = pl.BlockSpec(memory_space=pl.ANY)
    return pl.pallas_call(
        functools.partial(kernel, group_size, device_count),
        out_shape=(
            pltpu.VMEM((nodes, width), F32),
            pltpu.VMEM((queries, width), BF16),
        ),
        in_specs=[hbm] + [vmem] * 11 + [hbm, vmem, hbm, hbm, vmem, vmem] + [hbm] * 4 + [vmem],
        out_specs=(vmem, vmem),
        scratch_shapes=[
            pltpu.VMEM((nodes, width), BF16),
            pltpu.VMEM((nodes, width), BF16),
            pltpu.VMEM(msg_weight.shape, BF16),
            pltpu.VMEM(input_weight.shape, BF16),
            pltpu.VMEM(state_weight.shape, BF16),
            pltpu.VMEM(query_weight.shape, BF16),
            pltpu.VMEM(key_weight.shape, BF16),
            pltpu.VMEM(value_weight.shape, BF16),
            pltpu.VMEM(merge_weight.shape, BF16),
            pltpu.VMEM((device_count, 1, LANES), I32),
            pltpu.VMEM((device_count, 1, LANES), I32),
            pltpu.VMEM((device_count, LANES), I32),
            pltpu.VMEM((1, slots), F32),
            pltpu.VMEM((device_count, 8, width), BF16),
            pltpu.VMEM((device_count, 8, width), BF16),
            pltpu.VMEM((device_count, 8, width), BF16),
            pltpu.VMEM((device_count, 8, width), BF16),
            pltpu.VMEM((2 * events, slots), BF16),
            pltpu.VMEM((slots, 2 * events), BF16),
            pltpu.VMEM((2 * events, width), BF16),
            pltpu.VMEM((nodes, slots), BF16),
            pltpu.VMEM((nodes, LANES), F32),
            pltpu.VMEM((nodes, 3 * width), F32),
            pltpu.VMEM((2, group_size, queries, width), BF16),
            pltpu.VMEM((group_size, queries, LANES), I32),
            pltpu.VMEM((FAN, queries, LANES), BF16),
            pltpu.VMEM((HEADS * queries, width), BF16),
            pltpu.VMEM((2 * HEADS, queries, LANES), F32),
            pltpu.VMEM((HEADS, queries, LANES), F32),
            pltpu.VMEM((HEADS * queries, width), F32),
            pltpu.SemaphoreType.DMA((8,)),
            pltpu.SemaphoreType.DMA,
            pltpu.SemaphoreType.DMA((3,)),
            pltpu.SemaphoreType.DMA((3,)),
            pltpu.SemaphoreType.DMA((2,)),
            pltpu.SemaphoreType.DMA((2, group_size, 2)),
        ],
        compiler_params=pltpu.CompilerParams(
            collective_id=0, has_side_effects=True, vmem_limit_bytes=54 * 2**20
        ),
    )(
        memory,
        flat(source_owner),
        flat(target_owner),
        flat(source_row),
        flat(target_row),
        flat(event_time),
        flat(query_rows),
        flat(link_member),
        rows_of_lanes(link_slot),
        rows_of_lanes(link_delta),
        flat(frequency),
        flat(time_phase),
        msg_weight,
        flat(msg_bias),
        input_weight,
        state_weight,
        rows_of_lanes(input_bias),
        rows_of_lanes(state_bias),
        query_weight,
        key_weight,
        value_weight,
        merge_weight,
        merge_bias,
    )


def solution(mesh):
    both = ("group", "member")
    rows = P(both, None)
    flat = P(both)
    in_specs = (rows,) * 3 + (flat,) * 4 + (rows,) + (flat,) * 2 + (P(),) * 13
    return jax.shard_map(
        on_device, mesh=mesh, in_specs=in_specs, out_specs=(rows, rows), check_vma=False
    )
```

```python
import functools
import math

import jax
import jax.numpy as jnp
from jax import lax
from jax.experimental import pallas as pl
from jax.experimental.pallas import tpu as pltpu
from jax.sharding import PartitionSpec as P

MESH = pl.DeviceIdType.MESH
F32 = jnp.float32
BF16 = jnp.bfloat16
I32 = jnp.int32
HEADS = 2
FAN = 10
LANES = 128
NEG = -1e30


def iota(shape, dim):
    return lax.broadcasted_iota(I32, shape, dim)


def dot(a, b):
    return jnp.dot(a, b, preferred_element_type=F32)


def dot_t(a, b):
    return lax.dot_general(a, b, (((1,), (1,)), ((), ())), preferred_element_type=F32)


def cosine(x):
    turns = jnp.floor(x * (0.5 / math.pi) + 0.5)
    y = 0.5 * ((x - turns * 6.28125) - turns * (2.0 * math.pi - 6.28125))
    s = y * y
    p = 1.0 / 362880 - s * (1.0 / 39916800)
    p = -1.0 / 5040 + s * p
    p = 1.0 / 120 + s * p
    p = -1.0 / 6 + s * p
    sine = y + y * s * p
    return 1.0 - 2.0 * sine * sine


def column(row):
    n = row.shape[1]
    return jnp.sum(jnp.where(iota((n, n), 0) == iota((n, n), 1), row, 0.0), axis=1, keepdims=True)


def lanes_row(ref):
    return jnp.concatenate([ref[i : i + 1, :] for i in range(ref.shape[0])], axis=1)


def kernel(
    group_size,
    device_count,
    memory,
    s_owner,
    t_owner,
    s_row,
    t_row,
    e_time,
    q_rows,
    l_member,
    l_slot,
    l_delta,
    freq,
    phase,
    msg_w,
    msg_b,
    in_w,
    st_w,
    in_b,
    st_b,
    q_w,
    k_w,
    v_w,
    m_w,
    m_b,
    new_memory,
    embedding,
    mem_hi,
    mem_lo,
    msg_v,
    in_v,
    st_v,
    q_v,
    k_v,
    v_v,
    m_v,
    req_out,
    req_in,
    slot_row,
    xout,
    fetched,
    yout,
    inbound,
    pick,
    query_pick,
    place,
    msgs,
    back,
    touched,
    state,
    table,
    inverse,
    code,
    u_buf,
    cp,
    s_acc,
    acc,
    local_sem,
    out_sem,
    send_sem,
    recv_sem,
    hop_send,
    hop_recv,
):
    mem = new_memory
    group = lax.axis_index("group")
    member = lax.axis_index("member")
    me = group * group_size + member
    nodes, width = mem.shape
    in_bias = lanes_row(in_b)
    st_bias = lanes_row(st_b)
    events = s_row.shape[1]
    queries = q_rows.shape[1]
    slots = device_count * 8
    barrier = pltpu.get_barrier_semaphore()

    x_pos = lax.rem(lax.div(member, 2), 4)
    z_pos = lax.div(member, 8)
    core = lax.rem(member, 2)
    batch = lax.rem(group + z_pos + x_pos, 4)
    place_me = batch * 32 + group * 8 + z_pos * 2 + core

    def position(owner):
        y = jnp.right_shift(owner, 5)
        z = jnp.bitwise_and(jnp.right_shift(owner, 3), 3)
        x = jnp.bitwise_and(jnp.right_shift(owner, 1), 3)
        return jnp.bitwise_and(x + y + z, 3) * 32 + y * 8 + z * 2 + jnp.bitwise_and(owner, 1)

    def device(t):
        d = lax.rem(me + t, device_count)
        return d, {"group": lax.div(d, group_size), "member": lax.rem(d, group_size)}

    loads = [
        pltpu.make_async_copy(src, dst, local_sem.at[i])
        for i, (src, dst) in enumerate(
            [
                (memory, mem),
                (msg_w, msg_v),
                (st_w, st_v),
                (in_w, in_v),
                (q_w, q_v),
                (k_w, k_v),
                (v_w, v_v),
                (m_w, m_v),
            ]
        )
    ]
    for load in loads:
        load.start()

    def greet(t, _):
        _, dev = device(t + 1)
        pl.semaphore_signal(barrier, inc=1, device_id=dev, device_id_type=MESH)
        return 0

    lax.fori_loop(0, device_count - 1, greet, 0)

    places_row = []
    for role, owner_ref in enumerate((s_owner, t_owner)):
        own_row = position(owner_ref[...]).astype(F32)
        earlier = iota((events, events), 0) < iota((events, events), 1)
        same = column(own_row) == own_row
        rank_row = jnp.sum(jnp.where(same & earlier, 1.0, 0.0), axis=0, keepdims=True)
        places_row.append(own_row * 8.0 + (rank_row + 4.0 * role))
    place_row = jnp.concatenate(places_row, axis=1).astype(I32)
    wanted_row = jnp.concatenate([s_row[...], t_row[...]], axis=1).astype(F32) + 1.0

    lane_d = iota((device_count, LANES), 1)
    asked_out = jnp.zeros((device_count, LANES), F32)
    for slot in range(8):
        role_lanes = slice(0, events) if slot < 4 else slice(events, 2 * events)
        hit = place_row[:, role_lanes] == iota((device_count, events), 0) * 8 + slot
        asked = jnp.sum(jnp.where(hit, wanted_row[:, role_lanes], 0.0), axis=1, keepdims=True)
        asked_out = jnp.where(lane_d == slot, asked - 1.0, asked_out)
    req_out[:, 0, :] = asked_out.astype(I32)

    pl.semaphore_wait(barrier, device_count - 1)

    def exchange(src, dst, j, sem):
        def one(i, _):
            q = lax.rem(lax.rem(i, 16) * 7, 16)
            y = lax.rem(group + lax.div(q, 4), 4)
            z = lax.rem(z_pos + lax.rem(q, 4), 4)
            c = lax.rem(core + i + lax.div(i, 16), 2)
            k = lax.rem(batch + j, 4)
            x = lax.rem(k - y - z + 8, 4)
            place = k * 32 + y * 8 + z * 2 + c

            @pl.when(place != place_me)
            def _():
                pltpu.make_async_remote_copy(
                    src_ref=src.at[place],
                    dst_ref=dst.at[place_me],
                    send_sem=send_sem.at[sem],
                    recv_sem=recv_sem.at[sem, batch],
                    device_id={"group": y, "member": z * 8 + x * 2 + c},
                    device_id_type=MESH,
                ).start()

            return 0

        lax.fori_loop(0, 32, one, 0)

    def arrived(dst, which, own, sem):
        part = dst.at[pl.ds(0, 31 if own else 32)]
        pltpu.make_async_copy(part, part, recv_sem.at[sem, which]).wait()

    def sent(src, sem):
        part = src.at[pl.ds(0, device_count - 1)]
        pltpu.make_async_copy(part, part, send_sem.at[sem]).wait()

    def send_requests(j, _):
        exchange(req_out, req_in, j + 1, 0)
        return 0

    lax.fori_loop(0, 4, send_requests, 0)
    req_in[place_me] = req_out[place_me]

    loads[0].wait()

    def split(j, _):
        rows = pl.ds(j * LANES, LANES)
        x = mem[rows, :]
        hi = x.astype(BF16)
        mem_hi[rows, :] = hi
        mem_lo[rows, :] = (x - hi.astype(F32)).astype(BF16)
        return 0

    lax.fori_loop(0, nodes // LANES, split, 0)

    slot_of = lanes_row(l_slot)
    delta_of = lanes_row(l_delta)
    member_of = l_member[...]
    links = slot_of.shape[1]
    link_id = iota((queries, links), 1)
    first_link = iota((queries, links), 0) * FAN
    mine = (link_id >= first_link) & (link_id < first_link + FAN)
    link_f = iota((links, LANES), 0).astype(F32)
    link_k = link_f - FAN * jnp.floor((link_f + 0.5) * (1.0 / FAN))
    spread = jnp.where(link_k == iota((links, LANES), 1).astype(F32), 1.0, 0.0).astype(BF16)

    def arranged(row):
        return dot(jnp.where(mine, row.astype(F32), 0.0).astype(BF16), spread)

    lane_q = iota((queries, LANES), 1)
    live = lane_q < FAN
    slot_f = arranged(slot_of)
    member_f = arranged(member_of)
    high = jnp.right_shift(delta_of, 4)
    delta_f = arranged(high) * 16.0 + arranged(delta_of - high * 16)
    slot_i = jnp.where(live, slot_f, 0.0).astype(I32)
    member_i = jnp.where(live, member_f, -1.0).astype(I32)
    link_i = member_i * LANES + slot_i


    chunk = 2 * LANES
    peers = chunk // 8

    def asked_column(first, count):
        part = req_in[pl.ds(first, count), 0, :].astype(F32)
        spread_out = jnp.broadcast_to(part[:, None, :], (count, 8, LANES))
        mine_of = iota((count, 8, LANES), 1) == iota((count, 8, LANES), 2)
        column_of = jnp.sum(jnp.where(mine_of, spread_out, 0.0), axis=2, keepdims=True)
        return column_of.reshape(count * 8, 1)

    for step in range(1, 5):
        c = lax.rem(batch + 4 - step, 4)
        arrived(req_in, c, step == 4, 0)
        first = pl.multiple_of(c * peers, peers)
        asked = asked_column(first, peers)
        lane = iota((chunk, LANES), 1).astype(F32)
        hot = [
            jnp.where(asked == lane + float(b * LANES), 1.0, 0.0).astype(BF16)
            for b in range(nodes // LANES)
        ]
        rows = dot(jnp.concatenate(hot, axis=1), mem_hi[...])
        xout[pl.ds(first, peers)] = rows.reshape(peers, 8, width).astype(BF16)
        exchange(xout, fetched, 4 - step, 1)
    fetched[place_me] = xout[place_me]

    for role in range(2):
        place_col = column(places_row[role])
        for b in range(4):
            hit = (iota((events, chunk), 1) + b * chunk).astype(F32) == place_col
            pick[b, pl.ds(role * events, events), :] = jnp.where(hit, 1.0, 0.0).astype(BF16)

    def placing(j, _):
        hit = place_row == iota((LANES, 2 * events), 0) + j * LANES
        place[pl.ds(j * LANES, LANES), :] = jnp.where(hit, 1.0, 0.0).astype(BF16)
        return 0

    lax.fori_loop(0, slots // LANES, placing, 0)

    time_col = column(e_time[...].astype(F32))
    stamp = cosine(time_col * freq[...] + phase[...]).astype(BF16)
    for load in loads[1:]:
        load.wait()
    stamped = dot(stamp, msg_v[pl.ds(2 * width, LANES), :]) + msg_b[...]

    for b in range(slots // LANES):
        asked = asked_column(b * 16, 16)
        diagonal = iota((LANES, LANES), 0) == iota((LANES, LANES), 1)
        slot_row[:, pl.ds(b * LANES, LANES)] = jnp.sum(
            jnp.where(diagonal, asked, 0.0), axis=0, keepdims=True
        )

    def back_matrix(j, _):
        rows = pl.ds(j * LANES, LANES)
        node = (iota((LANES, slots), 0) + j * LANES).astype(F32)
        hot = jnp.where(slot_row[...] == node, 1.0, 0.0)
        back[rows, :] = hot.astype(BF16)
        touched[rows, :] = jnp.broadcast_to(
            jnp.sum(hot, axis=1, keepdims=True), (LANES, LANES)
        )
        return 0

    lax.fori_loop(0, nodes // LANES, back_matrix, 0)

    for k in range(FAN):
        code[k] = cosine(delta_f[:, k : k + 1] * freq[...] + phase[...]).astype(BF16)
    self_code = cosine(phase[...]).astype(BF16)

    def invert(b, _):
        node = lane_q + b * LANES
        found = jnp.full((queries, LANES), LANES - 1, I32)
        for k in range(FAN):
            found = jnp.where(link_i[:, k : k + 1] == node, k, found)
        inverse[b] = found
        return 0

    lax.fori_loop(0, group_size, invert, 0)

    sent(req_out, 0)

    pairs = jnp.zeros((2 * events, width), F32)
    for step in range(1, 5):
        c = lax.rem(batch + step, 4)
        arrived(fetched, c, step == 4, 1)
        rows = fetched[pl.ds(pl.multiple_of(c * peers, peers), peers)].reshape(chunk, width)
        pairs = pairs + dot(pick[c], rows)
    pairs = pairs.astype(BF16)
    swapped = jnp.concatenate([pairs[events:], pairs[:events]], axis=0)
    out = dot(pairs, msg_v[pl.ds(0, width), :]) + dot(swapped, msg_v[pl.ds(width, width), :])
    msgs[...] = jnp.maximum(out + jnp.concatenate([stamped, stamped], axis=0), 0.0).astype(BF16)

    def give_back(j, _):
        c = lax.rem(batch + j + 1, 4)
        rows = dot(place[pl.ds(c * chunk, chunk), :], msgs[...])
        yout[pl.ds(c * peers, peers)] = rows.reshape(peers, 8, width).astype(BF16)
        exchange(yout, inbound, j + 1, 2)
        return 0

    lax.fori_loop(0, slots // chunk, give_back, 0)
    inbound[place_me] = yout[place_me]

    query_col = column(q_rows[...].astype(F32))
    query_hot = jnp.where(
        iota((queries, nodes), 1).astype(F32) == query_col, 1.0, 0.0
    ).astype(BF16)
    query_touched = jnp.zeros((queries, 1), F32)
    for b in range(4):
        hit = jnp.where(slot_row[:, b * chunk : (b + 1) * chunk] == query_col, 1.0, 0.0)
        query_touched = query_touched + jnp.sum(hit, axis=1, keepdims=True)
        query_pick[b] = hit.astype(BF16)
    query_hi = dot(query_hot, mem_hi[...])
    query_mem = query_hi + dot(query_hot, mem_lo[...])
    query_state = dot(query_hi.astype(BF16), st_v[...]) + st_bias

    def states(j, _):
        rows = pl.ds(j * chunk, chunk)
        state[rows, :] = dot(mem_hi[rows, :], st_v[...]) + st_bias
        return 0

    lax.fori_loop(0, nodes // chunk, states, 0)

    sent(xout, 1)

    def cell(mean_msg, old, from_state):
        def part(i):
            return dot(mean_msg, in_v[:, i * width : (i + 1) * width]) + in_bias[:, i * width : (i + 1) * width]

        reset = jax.nn.sigmoid(part(0) + from_state[:, :width])
        update = jax.nn.sigmoid(part(1) + from_state[:, width : 2 * width])
        candidate = jnp.tanh(part(2) + reset * from_state[:, 2 * width :])
        return (1.0 - update) * candidate + update * old

    query_sum = jnp.zeros((queries, width), F32)
    for step in range(1, 5):
        c = lax.rem(batch + 4 - step, 4)
        arrived(inbound, c, step == 4, 2)
        rows = inbound[pl.ds(pl.multiple_of(c * peers, peers), peers)].reshape(chunk, width)
        query_sum = query_sum + dot(query_pick[c], rows)
    query_mean = (query_sum / jnp.maximum(query_touched, 1.0)).astype(BF16)
    fresh = cell(query_mean, query_mem, query_state)
    feats = jnp.where(query_touched > 0.0, fresh, query_mem).astype(BF16)

    def refresh(j, _):
        rows = pl.ds(j * LANES, LANES)
        count = touched[rows, 0:1]
        mean = dot(back[rows, :], inbound[...].reshape(slots, width)) / jnp.maximum(count, 1.0)
        old = mem[rows, :]
        new = cell(mean.astype(BF16), old, state[rows, :])
        mem[rows, :] = jnp.where(count > 0.0, new, old)
        return 0

    parity = lax.rem(member, 2)
    first_stride = 2 + 6 * parity
    second_stride = 8 - 6 * parity
    a_pos = lax.rem(lax.div(member, first_stride), 4)
    b_pos = lax.rem(lax.div(member, second_stride), 4)

    def at(da, db):
        return (
            lax.rem(a_pos + da + 4, 4) * first_stride
            + lax.rem(b_pos + db + 4, 4) * second_stride
            + parity
        )

    sibling = member + 1 - 2 * parity
    half = queries // 2

    for hop in range(2):
        rows_of = table.at[hop]
        sends = hop_send.at[hop]
        arrivals = hop_recv.at[hop]

        def piece(ref, which):
            return ref if which is None else ref.at[pl.ds(which * half, half)]

        def send(block, to, which=None):
            part = piece(rows_of.at[block], which)
            pltpu.make_async_remote_copy(
                src_ref=part,
                dst_ref=part,
                send_sem=sends,
                recv_sem=arrivals.at[block, 1 if which == 1 else 0],
                device_id={"member": to},
                device_id_type=MESH,
            ).start()

        def arrive(block, which=None):
            part = piece(rows_of.at[block], which)
            pltpu.make_async_copy(part, part, arrivals.at[block, 1 if which == 1 else 0]).wait()

        a_next, a_last, b_next, b_last = at(1, 0), at(-1, 0), at(0, 1), at(0, -1)

        rows_of[member] = feats
        for to, which in ((a_next, 0), (a_last, 1), (a_next, 1), (a_last, 0)):
            send(member, to, which)
        send(member, b_next, 0)
        send(member, b_last, 1)
        send(member, sibling)
        send(member, b_next, 1)
        send(member, b_last, 0)

        query_w = q_v.at[hop]
        key_w = k_v.at[hop]
        merge_w = m_v.at[hop]
        query_vec = dot(feats, query_w[pl.ds(0, width), :]) + dot(
            jnp.broadcast_to(self_code, (8, LANES)), query_w[pl.ds(width, LANES), :]
        )[0:1]
        merged_self = dot(feats, merge_w[pl.ds(width, width), :]) + m_b[hop : hop + 1, :]
        head = width // HEADS
        for h in range(HEADS):
            u = dot_t(
                (query_vec[:, h * head : (h + 1) * head] * (1.0 / math.sqrt(head))).astype(BF16),
                key_w[:, h * head : (h + 1) * head],
            )
            u_buf[pl.ds(h * queries, queries), :] = u[:, :width].astype(BF16)
            u_code = u[:, width:]
            c = jnp.full((queries, LANES), NEG, F32)
            for k in range(FAN):
                c = jnp.where(
                    lane_q == k,
                    jnp.sum(u_code * code[k].astype(F32), axis=1, keepdims=True),
                    c,
                )
            most = c
            for k in range(FAN):
                alike = (link_i == link_i[:, k : k + 1]) & live
                most = jnp.where(alike, jnp.maximum(most, c[:, k : k + 1]), most)
            total = jnp.zeros((queries, LANES), F32)
            for k in range(FAN):
                alike = (link_i == link_i[:, k : k + 1]) & live
                total = total + jnp.where(alike, jnp.exp(c[:, k : k + 1] - most), 0.0)
            cp[h] = jnp.where(live, most + jnp.log(jnp.where(live, total, 1.0)), NEG)
            cp[HEADS + h] = c
            s_acc[h] = jnp.zeros((queries, LANES), F32)
        acc[...] = jnp.zeros_like(acc)

        def attend(da, db):
            chip = lax.div(at(da, db), 2)
            arrive(2 * chip + 1 - parity)
            rows = rows_of[pl.ds(2 * chip, 2)].reshape(2 * queries, width)
            scores = dot_t(u_buf[...], rows)
            parts = []
            for h in range(HEADS):
                sides = []
                for side in range(2):
                    s = scores[
                        h * queries : (h + 1) * queries, side * queries : (side + 1) * queries
                    ]
                    bias = jnp.take_along_axis(cp[h], inverse[2 * chip + side], axis=1)
                    sides.append(jnp.exp(s + bias).astype(BF16))
                    picked = jnp.take_along_axis(s, slot_i, axis=1)
                    s_acc[h] = jnp.where(member_i == 2 * chip + side, picked, s_acc[h])
                parts.append(jnp.concatenate(sides, axis=1))
            acc[...] += dot(jnp.concatenate(parts, axis=0), rows)

        lax.fori_loop(hop * 4, hop * 4 + 2, refresh, 0)
        near, far, across = at(-1, 0), at(1, 0), at(2, 0)
        arrive(near, 0)
        send(near, a_next, 0)
        send(near, b_next, 0)
        arrive(far, 1)
        send(far, a_last, 1)
        send(far, b_last, 1)
        arrive(near, 1)
        send(near, b_last, 1)
        send(near, b_next, 1)
        arrive(far, 0)
        send(far, b_next, 0)
        send(far, b_last, 0)
        send(near, b_last, 0)
        send(far, b_next, 1)
        arrive(at(0, -1), 0)
        send(at(0, -1), b_next, 0)
        arrive(at(0, 1), 1)
        send(at(0, 1), b_last, 1)
        send(near, sibling)
        send(far, sibling)
        lax.fori_loop(hop * 4 + 2, hop * 4 + 3, refresh, 0)
        attend(0, 0)
        arrive(across, 0)
        send(across, b_next, 0)
        arrive(across, 1)
        send(across, b_last, 1)
        send(across, b_next, 1)
        send(across, b_last, 0)
        send(across, sibling)
        arrive(at(0, -1), 1)
        send(at(0, -1), sibling)
        arrive(at(0, 1), 0)
        send(at(0, 1), sibling)
        lax.fori_loop(hop * 4 + 3, hop * 4 + 4, refresh, 0)
        if hop == 1:
            pass
        attend(-1, 0)
        for da in (-1, 1):
            arrive(at(da, -1), 0)
            send(at(da, -1), b_next, 0)
            arrive(at(da, 1), 1)
            send(at(da, 1), b_last, 1)
        attend(1, 0)
        attend(0, -1)
        for da in (-1, 1):
            arrive(at(da, -1), 1)
            send(at(da, -1), sibling)
            arrive(at(da, 1), 0)
            send(at(da, 1), sibling)
        arrive(at(2, -1), 0)
        send(at(2, -1), b_next, 0)
        arrive(at(2, 1), 1)
        send(at(2, 1), b_last, 1)
        attend(0, 1)
        for which in range(2):
            arrive(at(0, 2), which)
        send(at(0, 2), sibling)
        arrive(at(2, -1), 1)
        send(at(2, -1), sibling)
        arrive(at(2, 1), 0)
        send(at(2, 1), sibling)
        for da in (-1, 1):
            for db in (-1, 1):
                attend(da, db)
        for da in (-1, 1):
            for which in range(2):
                arrive(at(da, 2), which)
            send(at(da, 2), sibling)
        attend(2, 0)
        attend(0, 2)
        for which in range(2):
            arrive(at(2, 2), which)
        send(at(2, 2), sibling)
        for da, db in ((2, -1), (2, 1), (-1, 2), (1, 2), (2, 2)):
            attend(da, db)

        value_w = v_v.at[hop]
        mixed = []
        for h in range(HEADS):
            w = jnp.where(live, jnp.exp(s_acc[h] + cp[HEADS + h]), 0.0)
            scale = 1.0 / jnp.sum(w, axis=1, keepdims=True)
            w = w * scale
            coded = jnp.zeros((queries, LANES), F32)
            for k in range(FAN):
                coded = coded + w[:, k : k + 1] * code[k].astype(F32)
            rows = (acc[pl.ds(h * queries, queries), :] * scale).astype(BF16)
            cols = slice(h * head, (h + 1) * head)
            mixed.append(
                dot(rows, value_w[pl.ds(0, width), cols])
                + dot(coded.astype(BF16), value_w[pl.ds(width, LANES), cols])
            )
        mixed = jnp.concatenate(mixed, axis=1).astype(BF16)
        merged = dot(mixed, merge_w[pl.ds(0, width), :]) + merged_self
        feats = jnp.maximum(merged, 0.0).astype(BF16)

        whole = rows_of.at[pl.ds(0, group_size - 1)]
        pltpu.make_async_copy(whole, whole, sends).wait()

    embedding[...] = feats
    sent(yout, 2)


def on_device(
    memory,
    source_owner,
    target_owner,
    source_row,
    target_row,
    event_time,
    query_rows,
    link_member,
    link_slot,
    link_delta,
    frequency,
    time_phase,
    msg_weight,
    msg_bias,
    input_weight,
    state_weight,
    input_bias,
    state_bias,
    query_weight,
    key_weight,
    value_weight,
    merge_weight,
    merge_bias,
):
    device_count = lax.axis_size(("group", "member"))
    group_size = lax.axis_size("member")
    nodes, width = memory.shape
    events = source_row.shape[0]
    queries = query_rows.shape[0]
    slots = device_count * 8

    def flat(x):
        return x.reshape(1, -1)

    def rows_of_lanes(x):
        return x.reshape(-1, LANES)

    vmem = pl.BlockSpec(memory_space=pltpu.VMEM)
    hbm = pl.BlockSpec(memory_space=pl.ANY)
    return pl.pallas_call(
        functools.partial(kernel, group_size, device_count),
        out_shape=(
            pltpu.VMEM((nodes, width), F32),
            pltpu.VMEM((queries, width), BF16),
        ),
        in_specs=[hbm] + [vmem] * 11 + [hbm, vmem, hbm, hbm, vmem, vmem] + [hbm] * 4 + [vmem],
        out_specs=(vmem, vmem),
        scratch_shapes=[
            pltpu.VMEM((nodes, width), BF16),
            pltpu.VMEM((nodes, width), BF16),
            pltpu.VMEM(msg_weight.shape, BF16),
            pltpu.VMEM(input_weight.shape, BF16),
            pltpu.VMEM(state_weight.shape, BF16),
            pltpu.VMEM(query_weight.shape, BF16),
            pltpu.VMEM(key_weight.shape, BF16),
            pltpu.VMEM(value_weight.shape, BF16),
            pltpu.VMEM(merge_weight.shape, BF16),
            pltpu.VMEM((device_count, 1, LANES), I32),
            pltpu.VMEM((device_count, 1, LANES), I32),
            pltpu.VMEM((1, slots), F32),
            pltpu.VMEM((device_count, 8, width), BF16),
            pltpu.VMEM((device_count, 8, width), BF16),
            pltpu.VMEM((device_count, 8, width), BF16),
            pltpu.VMEM((device_count, 8, width), BF16),
            pltpu.VMEM((4, 2 * events, slots // 4), BF16),
            pltpu.VMEM((4, queries, slots // 4), BF16),
            pltpu.VMEM((slots, 2 * events), BF16),
            pltpu.VMEM((2 * events, width), BF16),
            pltpu.VMEM((nodes, slots), BF16),
            pltpu.VMEM((nodes, LANES), F32),
            pltpu.VMEM((nodes, 3 * width), F32),
            pltpu.VMEM((2, group_size, queries, width), BF16),
            pltpu.VMEM((group_size, queries, LANES), I32),
            pltpu.VMEM((FAN, queries, LANES), BF16),
            pltpu.VMEM((HEADS * queries, width), BF16),
            pltpu.VMEM((2 * HEADS, queries, LANES), F32),
            pltpu.VMEM((HEADS, queries, LANES), F32),
            pltpu.VMEM((HEADS * queries, width), F32),
            pltpu.SemaphoreType.DMA((8,)),
            pltpu.SemaphoreType.DMA,
            pltpu.SemaphoreType.DMA((3,)),
            pltpu.SemaphoreType.DMA((3, 4)),
            pltpu.SemaphoreType.DMA((2,)),
            pltpu.SemaphoreType.DMA((2, group_size, 2)),
        ],
        compiler_params=pltpu.CompilerParams(
            collective_id=0, has_side_effects=True, vmem_limit_bytes=54 * 2**20
        ),
    )(
        memory,
        flat(source_owner),
        flat(target_owner),
        flat(source_row),
        flat(target_row),
        flat(event_time),
        flat(query_rows),
        flat(link_member),
        rows_of_lanes(link_slot),
        rows_of_lanes(link_delta),
        flat(frequency),
        flat(time_phase),
        msg_weight,
        flat(msg_bias),
        input_weight,
        state_weight,
        rows_of_lanes(input_bias),
        rows_of_lanes(state_bias),
        query_weight,
        key_weight,
        value_weight,
        merge_weight,
        merge_bias,
    )


def solution(mesh):
    both = ("group", "member")
    rows = P(both, None)
    flat = P(both)
    in_specs = (rows,) * 3 + (flat,) * 4 + (rows,) + (flat,) * 2 + (P(),) * 13
    return jax.shard_map(
        on_device, mesh=mesh, in_specs=in_specs, out_specs=(rows, rows), check_vma=False
    )
```

```python
import functools
import math

import jax
import jax.numpy as jnp
from jax import lax
from jax.experimental import pallas as pl
from jax.experimental.pallas import tpu as pltpu
from jax.sharding import PartitionSpec as P

MESH = pl.DeviceIdType.MESH
F32 = jnp.float32
BF16 = jnp.bfloat16
I32 = jnp.int32
HEADS = 2
FAN = 10
LANES = 128
NEG = -1e30


def iota(shape, dim):
    return lax.broadcasted_iota(I32, shape, dim)


def dot(a, b):
    return jnp.dot(a, b, preferred_element_type=F32)


def dot_t(a, b):
    return lax.dot_general(a, b, (((1,), (1,)), ((), ())), preferred_element_type=F32)


def cosine(x):
    turns = jnp.floor(x * (0.5 / math.pi) + 0.5)
    y = 0.5 * ((x - turns * 6.28125) - turns * (2.0 * math.pi - 6.28125))
    s = y * y
    p = 1.0 / 362880 - s * (1.0 / 39916800)
    p = -1.0 / 5040 + s * p
    p = 1.0 / 120 + s * p
    p = -1.0 / 6 + s * p
    sine = y + y * s * p
    return 1.0 - 2.0 * sine * sine


def column(row):
    n = row.shape[1]
    return jnp.sum(jnp.where(iota((n, n), 0) == iota((n, n), 1), row, 0.0), axis=1, keepdims=True)


def lanes_row(ref):
    return jnp.concatenate([ref[i : i + 1, :] for i in range(ref.shape[0])], axis=1)


def kernel(
    group_size,
    device_count,
    memory,
    s_owner,
    t_owner,
    s_row,
    t_row,
    e_time,
    q_rows,
    l_member,
    l_slot,
    l_delta,
    freq,
    phase,
    msg_w,
    msg_b,
    in_w,
    st_w,
    in_b,
    st_b,
    q_w,
    k_w,
    v_w,
    m_w,
    m_b,
    new_memory,
    embedding,
    mem_hi,
    mem_lo,
    msg_v,
    in_v,
    st_v,
    q_v,
    k_v,
    v_v,
    m_v,
    req_out,
    req_in,
    slot_row,
    xout,
    fetched,
    yout,
    inbound,
    pick,
    query_pick,
    place,
    msgs,
    back,
    touched,
    state,
    table,
    inverse,
    code,
    u_buf,
    cp,
    s_acc,
    acc,
    local_sem,
    out_sem,
    send_sem,
    recv_sem,
    hop_send,
    hop_recv,
):
    mem = new_memory
    group = lax.axis_index("group")
    member = lax.axis_index("member")
    me = group * group_size + member
    nodes, width = mem.shape
    in_bias = lanes_row(in_b)
    st_bias = lanes_row(st_b)
    events = s_row.shape[1]
    queries = q_rows.shape[1]
    slots = device_count * 8
    barrier = pltpu.get_barrier_semaphore()

    x_pos = lax.rem(lax.div(member, 2), 4)
    z_pos = lax.div(member, 8)
    core = lax.rem(member, 2)
    batch = lax.rem(group + z_pos + x_pos, 4)
    place_me = batch * 32 + group * 8 + z_pos * 2 + core

    def position(owner):
        y = jnp.right_shift(owner, 5)
        z = jnp.bitwise_and(jnp.right_shift(owner, 3), 3)
        x = jnp.bitwise_and(jnp.right_shift(owner, 1), 3)
        return jnp.bitwise_and(x + y + z, 3) * 32 + y * 8 + z * 2 + jnp.bitwise_and(owner, 1)

    def device(t):
        d = lax.rem(me + t, device_count)
        return d, {"group": lax.div(d, group_size), "member": lax.rem(d, group_size)}

    loads = [
        pltpu.make_async_copy(src, dst, local_sem.at[i])
        for i, (src, dst) in enumerate(
            [
                (memory, mem),
                (msg_w, msg_v),
                (st_w, st_v),
                (in_w, in_v),
                (q_w, q_v),
                (k_w, k_v),
                (v_w, v_v),
                (m_w, m_v),
            ]
        )
    ]
    for load in loads:
        load.start()

    def greet(t, _):
        _, dev = device(t + 1)
        pl.semaphore_signal(barrier, inc=1, device_id=dev, device_id_type=MESH)
        return 0

    lax.fori_loop(0, device_count - 1, greet, 0)

    places_row = []
    for role, owner_ref in enumerate((s_owner, t_owner)):
        own_row = position(owner_ref[...]).astype(F32)
        earlier = iota((events, events), 0) < iota((events, events), 1)
        same = column(own_row) == own_row
        rank_row = jnp.sum(jnp.where(same & earlier, 1.0, 0.0), axis=0, keepdims=True)
        places_row.append(own_row * 8.0 + (rank_row + 4.0 * role))
    place_row = jnp.concatenate(places_row, axis=1).astype(I32)
    wanted_row = jnp.concatenate([s_row[...], t_row[...]], axis=1).astype(F32) + 1.0

    lane_d = iota((device_count, LANES), 1)
    asked_out = jnp.zeros((device_count, LANES), F32)
    for slot in range(8):
        role_lanes = slice(0, events) if slot < 4 else slice(events, 2 * events)
        hit = place_row[:, role_lanes] == iota((device_count, events), 0) * 8 + slot
        asked = jnp.sum(jnp.where(hit, wanted_row[:, role_lanes], 0.0), axis=1, keepdims=True)
        asked_out = jnp.where(lane_d == slot, asked - 1.0, asked_out)
    req_out[:, 0, :] = asked_out.astype(I32)

    pl.semaphore_wait(barrier, device_count - 1)

    def exchange(src, dst, j, sem):
        def hops(q):
            steps = (q // 4, q % 4, (j - q // 4 - q % 4) % 4)
            return sum(min(s, 4 - s) for s in steps)

        order = sorted(range(16), key=lambda q: (-hops(q), q * 7 % 16))
        k = lax.rem(batch + j, 4)

        def one(i, rest):
            q = lax.rem(rest, 16)
            y = lax.rem(group + lax.div(q, 4), 4)
            z = lax.rem(z_pos + lax.rem(q, 4), 4)
            x = lax.rem(k - y - z + 8, 4)
            for flip in range(2):
                c = lax.rem(core + i + flip, 2)
                place = k * 32 + y * 8 + z * 2 + c

                def go():
                    pltpu.make_async_remote_copy(
                        src_ref=src.at[place],
                        dst_ref=dst.at[place_me],
                        send_sem=send_sem.at[sem],
                        recv_sem=recv_sem.at[sem, batch],
                        device_id={"group": y, "member": z * 8 + x * 2 + c},
                        device_id_type=MESH,
                    ).start()

                if j % 4 == 0:
                    pl.when(place != place_me)(go)
                else:
                    go()
            return lax.div(rest, 16)

        for first in range(0, 16, 4):
            packed = sum(q * 16**i for i, q in enumerate(order[first : first + 4]))
            lax.fori_loop(0, 4, one, jnp.int32(packed))

    def arrived(dst, which, own, sem):
        part = dst.at[pl.ds(0, 31 if own else 32)]
        pltpu.make_async_copy(part, part, recv_sem.at[sem, which]).wait()

    def sent(src, sem):
        part = src.at[pl.ds(0, device_count - 1)]
        pltpu.make_async_copy(part, part, send_sem.at[sem]).wait()

    for step in range(1, 5):
        exchange(req_out, req_in, step, 0)
    req_in[place_me] = req_out[place_me]

    loads[0].wait()

    def split(j, _):
        rows = pl.ds(j * LANES, LANES)
        x = mem[rows, :]
        hi = x.astype(BF16)
        mem_hi[rows, :] = hi
        return 0

    def remainder(j, _):
        rows = pl.ds(j * LANES, LANES)
        mem_lo[rows, :] = (mem[rows, :] - mem_hi[rows, :].astype(F32)).astype(BF16)
        return 0

    lax.fori_loop(0, nodes // LANES, split, 0)

    slot_of = lanes_row(l_slot)
    delta_of = lanes_row(l_delta)
    member_of = l_member[...]
    links = slot_of.shape[1]
    link_id = iota((queries, links), 1)
    first_link = iota((queries, links), 0) * FAN
    mine = (link_id >= first_link) & (link_id < first_link + FAN)
    link_f = iota((links, LANES), 0).astype(F32)
    link_k = link_f - FAN * jnp.floor((link_f + 0.5) * (1.0 / FAN))
    spread = jnp.where(link_k == iota((links, LANES), 1).astype(F32), 1.0, 0.0).astype(BF16)

    def arranged(row):
        return dot(jnp.where(mine, row.astype(F32), 0.0).astype(BF16), spread)

    lane_q = iota((queries, LANES), 1)
    live = lane_q < FAN
    slot_f = arranged(slot_of)
    member_f = arranged(member_of)
    high = jnp.right_shift(delta_of, 4)
    delta_f = arranged(high) * 16.0 + arranged(delta_of - high * 16)
    slot_i = jnp.where(live, slot_f, 0.0).astype(I32)
    member_i = jnp.where(live, member_f, -1.0).astype(I32)
    link_i = member_i * LANES + slot_i


    chunk = 2 * LANES
    peers = chunk // 8

    def asked_column(first, count):
        part = req_in[pl.ds(first, count), 0, :].astype(F32)
        spread_out = jnp.broadcast_to(part[:, None, :], (count, 8, LANES))
        mine_of = iota((count, 8, LANES), 1) == iota((count, 8, LANES), 2)
        column_of = jnp.sum(jnp.where(mine_of, spread_out, 0.0), axis=2, keepdims=True)
        return column_of.reshape(count * 8, 1)

    for step in range(1, 5):
        c = lax.rem(batch + 4 - step, 4)
        arrived(req_in, c, step == 4, 0)
        first = pl.multiple_of(c * peers, peers)
        asked = asked_column(first, peers)
        lane = iota((chunk, LANES), 1).astype(F32)
        hot = [
            jnp.where(asked == lane + float(b * LANES), 1.0, 0.0).astype(BF16)
            for b in range(nodes // LANES)
        ]
        rows = dot(jnp.concatenate(hot, axis=1), mem_hi[...])
        xout[pl.ds(first, peers)] = rows.reshape(peers, 8, width).astype(BF16)
        exchange(xout, fetched, 4 - step, 1)
    fetched[place_me] = xout[place_me]

    for role in range(2):
        place_col = column(places_row[role])
        for b in range(4):
            hit = (iota((events, chunk), 1) + b * chunk).astype(F32) == place_col
            pick[b, pl.ds(role * events, events), :] = jnp.where(hit, 1.0, 0.0).astype(BF16)

    def placing(j, _):
        hit = place_row == iota((LANES, 2 * events), 0) + j * LANES
        place[pl.ds(j * LANES, LANES), :] = jnp.where(hit, 1.0, 0.0).astype(BF16)
        return 0

    lax.fori_loop(0, slots // LANES, placing, 0)

    time_col = column(e_time[...].astype(F32))
    stamp = cosine(time_col * freq[...] + phase[...]).astype(BF16)
    for load in loads[1:]:
        load.wait()
    stamped = dot(stamp, msg_v[pl.ds(2 * width, LANES), :]) + msg_b[...]

    for b in range(slots // LANES):
        asked = asked_column(b * 16, 16)
        diagonal = iota((LANES, LANES), 0) == iota((LANES, LANES), 1)
        slot_row[:, pl.ds(b * LANES, LANES)] = jnp.sum(
            jnp.where(diagonal, asked, 0.0), axis=0, keepdims=True
        )

    def back_matrix(j, _):
        rows = pl.ds(j * LANES, LANES)
        node = (iota((LANES, slots), 0) + j * LANES).astype(F32)
        hot = jnp.where(slot_row[...] == node, 1.0, 0.0)
        back[rows, :] = hot.astype(BF16)
        touched[rows, :] = jnp.broadcast_to(
            jnp.sum(hot, axis=1, keepdims=True), (LANES, LANES)
        )
        return 0

    lax.fori_loop(0, nodes // LANES, back_matrix, 0)

    for k in range(FAN):
        code[k] = cosine(delta_f[:, k : k + 1] * freq[...] + phase[...]).astype(BF16)
    self_code = cosine(phase[...]).astype(BF16)

    def invert(b, _):
        node = lane_q + b * LANES
        found = jnp.full((queries, LANES), LANES - 1, I32)
        for k in range(FAN):
            found = jnp.where(link_i[:, k : k + 1] == node, k, found)
        inverse[b] = found
        return 0

    lax.fori_loop(0, group_size, invert, 0)

    sent(req_out, 0)

    pairs = jnp.zeros((2 * events, width), F32)
    for step in range(1, 5):
        c = lax.rem(batch + step, 4)
        arrived(fetched, c, step == 4, 1)
        rows = fetched[pl.ds(pl.multiple_of(c * peers, peers), peers)].reshape(chunk, width)
        pairs = pairs + dot(pick[c], rows)
    pairs = pairs.astype(BF16)
    swapped = jnp.concatenate([pairs[events:], pairs[:events]], axis=0)
    out = dot(pairs, msg_v[pl.ds(0, width), :]) + dot(swapped, msg_v[pl.ds(width, width), :])
    msgs[...] = jnp.maximum(out + jnp.concatenate([stamped, stamped], axis=0), 0.0).astype(BF16)

    for step in range(1, 5):
        c = lax.rem(batch + step, 4)
        rows = dot(place[pl.ds(pl.multiple_of(c * chunk, chunk), chunk), :], msgs[...])
        yout[pl.ds(c * peers, peers)] = rows.reshape(peers, 8, width).astype(BF16)
        exchange(yout, inbound, step, 2)

    inbound[place_me] = yout[place_me]

    lax.fori_loop(0, nodes // LANES, remainder, 0)
    query_col = column(q_rows[...].astype(F32))
    query_hot = jnp.where(
        iota((queries, nodes), 1).astype(F32) == query_col, 1.0, 0.0
    ).astype(BF16)
    query_touched = jnp.zeros((queries, 1), F32)
    for b in range(4):
        hit = jnp.where(slot_row[:, b * chunk : (b + 1) * chunk] == query_col, 1.0, 0.0)
        query_touched = query_touched + jnp.sum(hit, axis=1, keepdims=True)
        query_pick[b] = hit.astype(BF16)
    query_hi = dot(query_hot, mem_hi[...])
    query_mem = query_hi + dot(query_hot, mem_lo[...])
    query_state = dot(query_hi.astype(BF16), st_v[...]) + st_bias

    def states(j, _):
        rows = pl.ds(j * chunk, chunk)
        state[rows, :] = dot(mem_hi[rows, :], st_v[...]) + st_bias
        return 0

    lax.fori_loop(0, nodes // chunk, states, 0)

    sent(xout, 1)

    def cell(mean_msg, old, from_state):
        def part(i):
            return dot(mean_msg, in_v[:, i * width : (i + 1) * width]) + in_bias[:, i * width : (i + 1) * width]

        reset = jax.nn.sigmoid(part(0) + from_state[:, :width])
        update = jax.nn.sigmoid(part(1) + from_state[:, width : 2 * width])
        candidate = jnp.tanh(part(2) + reset * from_state[:, 2 * width :])
        return (1.0 - update) * candidate + update * old

    query_sum = jnp.zeros((queries, width), F32)
    for step in range(1, 5):
        c = lax.rem(batch + 4 - step, 4)
        arrived(inbound, c, step == 4, 2)
        rows = inbound[pl.ds(pl.multiple_of(c * peers, peers), peers)].reshape(chunk, width)
        query_sum = query_sum + dot(query_pick[c], rows)
    query_mean = (query_sum / jnp.maximum(query_touched, 1.0)).astype(BF16)
    fresh = cell(query_mean, query_mem, query_state)
    feats = jnp.where(query_touched > 0.0, fresh, query_mem).astype(BF16)

    def refresh(j, _):
        rows = pl.ds(j * LANES, LANES)
        count = touched[rows, 0:1]
        mean = dot(back[rows, :], inbound[...].reshape(slots, width)) / jnp.maximum(count, 1.0)
        old = mem[rows, :]
        new = cell(mean.astype(BF16), old, state[rows, :])
        mem[rows, :] = jnp.where(count > 0.0, new, old)
        return 0

    parity = lax.rem(member, 2)
    first_stride = 2 + 6 * parity
    second_stride = 8 - 6 * parity
    a_pos = lax.rem(lax.div(member, first_stride), 4)
    b_pos = lax.rem(lax.div(member, second_stride), 4)

    def at(da, db):
        return (
            lax.rem(a_pos + da + 4, 4) * first_stride
            + lax.rem(b_pos + db + 4, 4) * second_stride
            + parity
        )

    sibling = member + 1 - 2 * parity
    half = queries // 2

    for hop in range(2):
        rows_of = table.at[hop]
        sends = hop_send.at[hop]
        arrivals = hop_recv.at[hop]

        def piece(ref, which):
            return ref if which is None else ref.at[pl.ds(which * half, half)]

        def send(block, to, which=None):
            part = piece(rows_of.at[block], which)
            pltpu.make_async_remote_copy(
                src_ref=part,
                dst_ref=part,
                send_sem=sends,
                recv_sem=arrivals.at[block, 1 if which == 1 else 0],
                device_id={"member": to},
                device_id_type=MESH,
            ).start()

        def arrive(block, which=None):
            part = piece(rows_of.at[block], which)
            pltpu.make_async_copy(part, part, arrivals.at[block, 1 if which == 1 else 0]).wait()

        a_next, a_last, b_next, b_last = at(1, 0), at(-1, 0), at(0, 1), at(0, -1)

        rows_of[member] = feats
        for to, which in ((a_next, 0), (a_last, 1), (a_next, 1), (a_last, 0)):
            send(member, to, which)
        send(member, b_next, 0)
        send(member, b_last, 1)
        send(member, sibling)
        send(member, b_next, 1)
        send(member, b_last, 0)

        query_w = q_v.at[hop]
        key_w = k_v.at[hop]
        merge_w = m_v.at[hop]
        query_vec = dot(feats, query_w[pl.ds(0, width), :]) + dot(
            jnp.broadcast_to(self_code, (8, LANES)), query_w[pl.ds(width, LANES), :]
        )[0:1]
        merged_self = dot(feats, merge_w[pl.ds(width, width), :]) + m_b[hop : hop + 1, :]
        head = width // HEADS
        for h in range(HEADS):
            u = dot_t(
                (query_vec[:, h * head : (h + 1) * head] * (1.0 / math.sqrt(head))).astype(BF16),
                key_w[:, h * head : (h + 1) * head],
            )
            u_buf[pl.ds(h * queries, queries), :] = u[:, :width].astype(BF16)
            u_code = u[:, width:]
            c = jnp.full((queries, LANES), NEG, F32)
            for k in range(FAN):
                c = jnp.where(
                    lane_q == k,
                    jnp.sum(u_code * code[k].astype(F32), axis=1, keepdims=True),
                    c,
                )
            most = c
            for k in range(FAN):
                alike = (link_i == link_i[:, k : k + 1]) & live
                most = jnp.where(alike, jnp.maximum(most, c[:, k : k + 1]), most)
            total = jnp.zeros((queries, LANES), F32)
            for k in range(FAN):
                alike = (link_i == link_i[:, k : k + 1]) & live
                total = total + jnp.where(alike, jnp.exp(c[:, k : k + 1] - most), 0.0)
            cp[h] = jnp.where(live, most + jnp.log(jnp.where(live, total, 1.0)), NEG)
            cp[HEADS + h] = c
            s_acc[h] = jnp.zeros((queries, LANES), F32)
        acc[...] = jnp.zeros_like(acc)

        def attend(da, db):
            chip = lax.div(at(da, db), 2)
            arrive(2 * chip + 1 - parity)
            rows = rows_of[pl.ds(2 * chip, 2)].reshape(2 * queries, width)
            scores = dot_t(u_buf[...], rows)
            parts = []
            for h in range(HEADS):
                sides = []
                for side in range(2):
                    s = scores[
                        h * queries : (h + 1) * queries, side * queries : (side + 1) * queries
                    ]
                    bias = jnp.take_along_axis(cp[h], inverse[2 * chip + side], axis=1)
                    sides.append(jnp.exp(s + bias).astype(BF16))
                    picked = jnp.take_along_axis(s, slot_i, axis=1)
                    s_acc[h] = jnp.where(member_i == 2 * chip + side, picked, s_acc[h])
                parts.append(jnp.concatenate(sides, axis=1))
            acc[...] += dot(jnp.concatenate(parts, axis=0), rows)

        lax.fori_loop(hop * 4, hop * 4 + 2, refresh, 0)
        near, far, across = at(-1, 0), at(1, 0), at(2, 0)
        arrive(near, 0)
        send(near, a_next, 0)
        send(near, b_next, 0)
        arrive(far, 1)
        send(far, a_last, 1)
        send(far, b_last, 1)
        arrive(near, 1)
        send(near, b_last, 1)
        send(near, b_next, 1)
        arrive(far, 0)
        send(far, b_next, 0)
        send(far, b_last, 0)
        send(near, b_last, 0)
        send(far, b_next, 1)
        arrive(at(0, -1), 0)
        send(at(0, -1), b_next, 0)
        arrive(at(0, 1), 1)
        send(at(0, 1), b_last, 1)
        send(near, sibling)
        send(far, sibling)
        lax.fori_loop(hop * 4 + 2, hop * 4 + 3, refresh, 0)
        attend(0, 0)
        arrive(across, 0)
        send(across, b_next, 0)
        arrive(across, 1)
        send(across, b_last, 1)
        send(across, b_next, 1)
        send(across, b_last, 0)
        send(across, sibling)
        arrive(at(0, -1), 1)
        send(at(0, -1), sibling)
        arrive(at(0, 1), 0)
        send(at(0, 1), sibling)
        lax.fori_loop(hop * 4 + 3, hop * 4 + 4, refresh, 0)
        if hop == 1:
            pass
        attend(-1, 0)
        for da in (-1, 1):
            arrive(at(da, -1), 0)
            send(at(da, -1), b_next, 0)
            arrive(at(da, 1), 1)
            send(at(da, 1), b_last, 1)
        attend(1, 0)
        attend(0, -1)
        for da in (-1, 1):
            arrive(at(da, -1), 1)
            send(at(da, -1), sibling)
            arrive(at(da, 1), 0)
            send(at(da, 1), sibling)
        arrive(at(2, -1), 0)
        send(at(2, -1), b_next, 0)
        arrive(at(2, 1), 1)
        send(at(2, 1), b_last, 1)
        attend(0, 1)
        for which in range(2):
            arrive(at(0, 2), which)
        send(at(0, 2), sibling)
        arrive(at(2, -1), 1)
        send(at(2, -1), sibling)
        arrive(at(2, 1), 0)
        send(at(2, 1), sibling)
        for da in (-1, 1):
            for db in (-1, 1):
                attend(da, db)
        for da in (-1, 1):
            for which in range(2):
                arrive(at(da, 2), which)
            send(at(da, 2), sibling)
        attend(2, 0)
        attend(0, 2)
        for which in range(2):
            arrive(at(2, 2), which)
        send(at(2, 2), sibling)
        for da, db in ((2, -1), (2, 1), (-1, 2), (1, 2), (2, 2)):
            attend(da, db)

        value_w = v_v.at[hop]
        mixed = []
        for h in range(HEADS):
            w = jnp.where(live, jnp.exp(s_acc[h] + cp[HEADS + h]), 0.0)
            scale = 1.0 / jnp.sum(w, axis=1, keepdims=True)
            w = w * scale
            coded = jnp.zeros((queries, LANES), F32)
            for k in range(FAN):
                coded = coded + w[:, k : k + 1] * code[k].astype(F32)
            rows = (acc[pl.ds(h * queries, queries), :] * scale).astype(BF16)
            cols = slice(h * head, (h + 1) * head)
            mixed.append(
                dot(rows, value_w[pl.ds(0, width), cols])
                + dot(coded.astype(BF16), value_w[pl.ds(width, LANES), cols])
            )
        mixed = jnp.concatenate(mixed, axis=1).astype(BF16)
        merged = dot(mixed, merge_w[pl.ds(0, width), :]) + merged_self
        feats = jnp.maximum(merged, 0.0).astype(BF16)

        whole = rows_of.at[pl.ds(0, group_size - 1)]
        pltpu.make_async_copy(whole, whole, sends).wait()

    embedding[...] = feats
    sent(yout, 2)


def on_device(
    memory,
    source_owner,
    target_owner,
    source_row,
    target_row,
    event_time,
    query_rows,
    link_member,
    link_slot,
    link_delta,
    frequency,
    time_phase,
    msg_weight,
    msg_bias,
    input_weight,
    state_weight,
    input_bias,
    state_bias,
    query_weight,
    key_weight,
    value_weight,
    merge_weight,
    merge_bias,
):
    device_count = lax.axis_size(("group", "member"))
    group_size = lax.axis_size("member")
    nodes, width = memory.shape
    events = source_row.shape[0]
    queries = query_rows.shape[0]
    slots = device_count * 8

    def flat(x):
        return x.reshape(1, -1)

    def rows_of_lanes(x):
        return x.reshape(-1, LANES)

    vmem = pl.BlockSpec(memory_space=pltpu.VMEM)
    hbm = pl.BlockSpec(memory_space=pl.ANY)
    return pl.pallas_call(
        functools.partial(kernel, group_size, device_count),
        out_shape=(
            pltpu.VMEM((nodes, width), F32),
            pltpu.VMEM((queries, width), BF16),
        ),
        in_specs=[hbm] + [vmem] * 11 + [hbm, vmem, hbm, hbm, vmem, vmem] + [hbm] * 4 + [vmem],
        out_specs=(vmem, vmem),
        scratch_shapes=[
            pltpu.VMEM((nodes, width), BF16),
            pltpu.VMEM((nodes, width), BF16),
            pltpu.VMEM(msg_weight.shape, BF16),
            pltpu.VMEM(input_weight.shape, BF16),
            pltpu.VMEM(state_weight.shape, BF16),
            pltpu.VMEM(query_weight.shape, BF16),
            pltpu.VMEM(key_weight.shape, BF16),
            pltpu.VMEM(value_weight.shape, BF16),
            pltpu.VMEM(merge_weight.shape, BF16),
            pltpu.VMEM((device_count, 1, LANES), I32),
            pltpu.VMEM((device_count, 1, LANES), I32),
            pltpu.VMEM((1, slots), F32),
            pltpu.VMEM((device_count, 8, width), BF16),
            pltpu.VMEM((device_count, 8, width), BF16),
            pltpu.VMEM((device_count, 8, width), BF16),
            pltpu.VMEM((device_count, 8, width), BF16),
            pltpu.VMEM((4, 2 * events, slots // 4), BF16),
            pltpu.VMEM((4, queries, slots // 4), BF16),
            pltpu.VMEM((slots, 2 * events), BF16),
            pltpu.VMEM((2 * events, width), BF16),
            pltpu.VMEM((nodes, slots), BF16),
            pltpu.VMEM((nodes, LANES), F32),
            pltpu.VMEM((nodes, 3 * width), F32),
            pltpu.VMEM((2, group_size, queries, width), BF16),
            pltpu.VMEM((group_size, queries, LANES), I32),
            pltpu.VMEM((FAN, queries, LANES), BF16),
            pltpu.VMEM((HEADS * queries, width), BF16),
            pltpu.VMEM((2 * HEADS, queries, LANES), F32),
            pltpu.VMEM((HEADS, queries, LANES), F32),
            pltpu.VMEM((HEADS * queries, width), F32),
            pltpu.SemaphoreType.DMA((8,)),
            pltpu.SemaphoreType.DMA,
            pltpu.SemaphoreType.DMA((3,)),
            pltpu.SemaphoreType.DMA((3, 4)),
            pltpu.SemaphoreType.DMA((2,)),
            pltpu.SemaphoreType.DMA((2, group_size, 2)),
        ],
        compiler_params=pltpu.CompilerParams(
            collective_id=0, has_side_effects=True, vmem_limit_bytes=54 * 2**20
        ),
    )(
        memory,
        flat(source_owner),
        flat(target_owner),
        flat(source_row),
        flat(target_row),
        flat(event_time),
        flat(query_rows),
        flat(link_member),
        rows_of_lanes(link_slot),
        rows_of_lanes(link_delta),
        flat(frequency),
        flat(time_phase),
        msg_weight,
        flat(msg_bias),
        input_weight,
        state_weight,
        rows_of_lanes(input_bias),
        rows_of_lanes(state_bias),
        query_weight,
        key_weight,
        value_weight,
        merge_weight,
        merge_bias,
    )


def solution(mesh):
    both = ("group", "member")
    rows = P(both, None)
    flat = P(both)
    in_specs = (rows,) * 3 + (flat,) * 4 + (rows,) + (flat,) * 2 + (P(),) * 13
    return jax.shard_map(
        on_device, mesh=mesh, in_specs=in_specs, out_specs=(rows, rows), check_vma=False
    )
```
